128 devices in a mesh: dp: 16 (over x, z), seq: 8 (over y, core).
Axes of the slice: x: 4, y: 4, z: 4, core: 2. Of those that a mesh axis runs over, the one named last changes fastest.
Arguments:
- grad_out: bfloat16 [16, 1024, 4096], P('dp', 'seq'), may hold values from -6 to 6
- queries: bfloat16 [16, 1024, 4096], P('dp', 'seq'), may hold values from -45 to 45
- keys: bfloat16 [16, 1024, 1024], P('dp', 'seq'), may hold values from -4 to 4
- values: bfloat16 [16, 1024, 1024], P('dp', 'seq'), may hold values from -6 to 6
- out_weight: bfloat16 [4096, 4096], P('seq'), may hold values from -0.09375 to 0.09375
- doc_starts: int32 [16, 8], P('dp'), may hold values from 0 to 1020, as said below
Outputs:
- grad_queries: bfloat16 [16, 1024, 4096], P('dp', 'seq')
- grad_keys: bfloat16 [16, 1024, 1024], P('dp', 'seq')
- grad_values: bfloat16 [16, 1024, 1024], P('dp', 'seq')
- grad_weight: float32 [4096, 4096], P('seq', 'dp')
The draws below stay inside these ranges and needn't reach their ends.
Inputs may be any that keep to these rules, and one draw needn't show every extreme that they name: `doc_starts`: each row strictly increases, holds multiples of 4, begins with 0 and ends with 1020.
All inputs are finite; a program needn't handle non-finite values.
Results may differ from the reference program's by a relative error of at most 0.015.
Values may be sent and summed in bfloat16 or wider, within the bound.
A program may use at most 128 MiB of HBM per device.

```python
import math
import jax
import jax.numpy as jnp
from jax import lax

HEADS = 32
KV_HEADS = 8
HEAD_DIM = 128
D = 4096
SEQ_LEN = 1024
NDOC = 8
SEQS = 16


def pair_draw(key):
    base = jax.random.fold_in(key, 7)
    key_first, key_second = jax.random.split(base, 2)
    keys_out = jax.random.truncated_normal(key_first, -4.0, 4.0, (SEQS, SEQ_LEN, KV_HEADS * HEAD_DIM), jnp.float32)
    query_out = jax.random.truncated_normal(key_second, -4.0, 4.0, (SEQS, SEQ_LEN, HEADS * HEAD_DIM), jnp.float32)
    return (query_out, keys_out)


def draw_queries(key, part):
    return pair_draw(key)[0].astype(jnp.bfloat16)


def draw_keys(key, part):
    return pair_draw(key)[1].astype(jnp.bfloat16)


def draw_doc_starts(key, part):

    def one_row(index):
        chosen = jax.random.permutation(jax.random.fold_in(key, index), SEQ_LEN // 4 - 2)[:NDOC - 2] + 1
        middle = (jnp.sort(chosen) * 4).astype(jnp.int32)
        return jnp.concatenate([jnp.zeros((1,), jnp.int32), middle, jnp.full((1,), SEQ_LEN - 4, jnp.int32)])
    return jax.vmap(one_row)(jnp.arange(SEQS))


def spiked(result, own_key, source, target, blocks, factor):
    owner, partner = [(jnp.arange(result.shape[dim]) // (result.shape[dim] // blocks)).reshape([-1 if axis == dim else 1 for axis in range(result.ndim)]) for dim in (source, target)]
    chosen = jax.random.permutation(own_key, blocks)[partner]
    strong = (owner == chosen) | (owner == (partner + blocks // 2) % blocks)
    return jnp.where(strong, factor * result, result)


def steps_of(stream_key, dims, shards, least, high):
    def one(dim, blocks):
        steps = jax.random.uniform(jax.random.fold_in(jax.random.fold_in(stream_key, 6), dim), (blocks,), jnp.float32, least / len(shards), high / len(shards))
        return jnp.repeat(jnp.exp(steps), dims[dim] // blocks).reshape((-1,) + (1,) * (len(dims) - dim - 1))

    gain = one(*shards[0])
    for cut in shards[1:]:
        gain = gain * one(*cut)
    return gain


def bell_draw(stream_key, dims, scale, bound, cuts=(), held_as=jnp.bfloat16):
    level = steps_of(stream_key, dims, cuts, -0.22, 0.18) if cuts else 1.0
    entries = jax.random.normal(stream_key, dims, jnp.float32) * scale * level
    return jnp.minimum(jnp.maximum(entries, -bound), bound).astype(held_as)


def heavy_noise(stream_key, dims, width, reach, pieces, heavy, kind=jnp.bfloat16):
    drawn = width * jax.random.normal(stream_key, dims, jnp.float32)
    if pieces:
        drawn = drawn * steps_of(stream_key, dims, pieces, -0.22, 0.18)
    return jnp.clip(spiked(drawn, jax.random.fold_in(stream_key, 3), *heavy), -reach, reach).astype(kind)


def setup_inputs(seed: int = 0) -> dict:
    seeds = jax.random.split(jax.random.key(seed), 7)
    return {
        "grad_out": heavy_noise(seeds[0], (SEQS, SEQ_LEN, D), 1.0, 6.0, ((0, 16), (1, 8)), (0, 2, 16, 2.0)),
        "queries": draw_queries(jax.random.fold_in(seeds[6], 71), 0),
        "keys": draw_keys(jax.random.fold_in(seeds[6], 71), 0),
        "values": bell_draw(seeds[3], (SEQS, SEQ_LEN, KV_HEADS * HEAD_DIM), 1.0, 6.0, ((0, 16), (1, 8))),
        "out_weight": bell_draw(seeds[4], (D, D), D ** -0.5, 0.09375, ((0, 8),)),
        "doc_starts": draw_doc_starts(jax.random.fold_in(seeds[6], 71), 0),
    }


def visible(starts, first_row, row_count, key_count):
    rows_pos = first_row + jnp.arange(row_count, dtype=jnp.int32)
    keys_pos = jnp.arange(key_count, dtype=jnp.int32)
    opening = lax.optimization_barrier(jnp.max(jnp.where(starts[None, :] <= rows_pos[:, None], starts[None, :], 0), axis=1))
    return (keys_pos[None, :] >= opening[:, None]) & (keys_pos[None, :] <= rows_pos[:, None])

def weights_of(query_rows, key_rows, allowed, scale):
    scores = lax.dot_general(query_rows, key_rows, (((1,), (1,)), ((), ())), preferred_element_type=jnp.float32) * scale
    scores = jnp.where(allowed, scores, -1e+30)
    highest = lax.optimization_barrier(jnp.max(scores, axis=1, keepdims=True))
    raised = jnp.exp(scores - highest)
    return raised / lax.optimization_barrier(jnp.sum(raised, axis=1, keepdims=True))

def attend(query_all, key_all, value_all, starts, group, head_dim, block, trimmed):
    length = query_all.shape[0]
    scale = 1.0 / math.sqrt(head_dim)
    columns = []
    for member in range(query_all.shape[1] // head_dim):
        shared = member // group
        query_head = query_all[:, member * head_dim:(member + 1) * head_dim]
        key_head = key_all[:, shared * head_dim:(shared + 1) * head_dim]
        value_head = value_all[:, shared * head_dim:(shared + 1) * head_dim]
        blocks = []
        for section in range(length // block):
            first = section * block
            ending = first + block if trimmed else length
            allowed = visible(starts, first, block, ending)
            probs = weights_of(query_head[first:first + block], key_head[:ending], allowed, scale)
            blocks.append(jnp.dot(probs.astype(jnp.bfloat16), value_head[:ending], preferred_element_type=jnp.float32).astype(jnp.bfloat16))
        columns.append(jnp.concatenate(blocks, axis=0))
    return jnp.concatenate(columns, axis=1)

def attend_back(query_all, key_all, value_all, out_all, grad_all, starts, group, head_dim, block, trimmed):
    length = query_all.shape[0]
    scale = 1.0 / math.sqrt(head_dim)
    shared_count = key_all.shape[1] // head_dim
    key_grads = [jnp.zeros((length, head_dim), jnp.float32) for shared in range(shared_count)]
    value_grads = [jnp.zeros((length, head_dim), jnp.float32) for shared in range(shared_count)]
    query_grads = []
    for member in range(query_all.shape[1] // head_dim):
        shared = member // group
        lo_col = member * head_dim
        query_head = query_all[:, lo_col:lo_col + head_dim]
        key_head = key_all[:, shared * head_dim:(shared + 1) * head_dim]
        value_head = value_all[:, shared * head_dim:(shared + 1) * head_dim]
        blocks = []
        for section in range(length // block):
            first = section * block
            ending = first + block if trimmed else length
            allowed = visible(starts, first, block, ending)
            query_rows = query_head[first:first + block]
            probs = weights_of(query_rows, key_head[:ending], allowed, scale)
            probs_low = probs.astype(jnp.bfloat16)
            grad_rows = grad_all[first:first + block, lo_col:lo_col + head_dim]
            out_rows = out_all[first:first + block, lo_col:lo_col + head_dim]
            value_grads[shared] = value_grads[shared].at[:ending].add(lax.dot_general(probs_low, grad_rows, (((0,), (0,)), ((), ())), preferred_element_type=jnp.float32))
            grad_probs = lax.dot_general(grad_rows, value_head[:ending], (((1,), (1,)), ((), ())), preferred_element_type=jnp.float32)
            delta = lax.optimization_barrier(jnp.sum(grad_rows.astype(jnp.float32) * out_rows.astype(jnp.float32), axis=1, keepdims=True))
            grad_scores = (probs * (grad_probs - delta)).astype(jnp.bfloat16)
            blocks.append((jnp.dot(grad_scores, key_head[:ending], preferred_element_type=jnp.float32) * scale).astype(jnp.bfloat16))
            key_grads[shared] = key_grads[shared].at[:ending].add(lax.dot_general(grad_scores, query_rows, (((0,), (0,)), ((), ())), preferred_element_type=jnp.float32) * scale)
        query_grads.append(jnp.concatenate(blocks, axis=0))
    grad_q = jnp.concatenate(query_grads, axis=1)
    grad_k = jnp.concatenate(key_grads, axis=1).astype(jnp.bfloat16)
    grad_v = jnp.concatenate(value_grads, axis=1).astype(jnp.bfloat16)
    return (grad_q, grad_k, grad_v)

def reference(grad_out, queries, keys, values, out_weight, doc_starts):
    group = HEADS // KV_HEADS
    block = min(512, SEQ_LEN)

    def one_sequence(weight_sum, inputs):
        grad_rows, query_all, key_all, value_all, starts = inputs
        out_all = attend(query_all, key_all, value_all, starts, group, HEAD_DIM, block, False)
        grad_attn = lax.dot_general(grad_rows, out_weight, (((1,), (1,)), ((), ())), preferred_element_type=jnp.float32).astype(jnp.bfloat16)
        weight_sum = weight_sum + lax.dot_general(out_all, grad_rows, (((0,), (0,)), ((), ())), preferred_element_type=jnp.float32)
        grads = attend_back(query_all, key_all, value_all, out_all, grad_attn, starts, group, HEAD_DIM, block, False)
        return (weight_sum, grads)
    weight_sum, grads = lax.scan(one_sequence, jnp.zeros((D, D), jnp.float32), (grad_out, queries, keys, values, doc_starts))
    scaled = weight_sum * (1.0 / math.sqrt(SEQS * SEQ_LEN))
    return (grads[0], grads[1], grads[2], scaled)
```

```python
import math

import jax
import jax.numpy as jnp
from jax import lax
from jax.experimental import pallas as pl
from jax.experimental.pallas import tpu as pltpu
from jax.sharding import PartitionSpec as P

MESH = pl.DeviceIdType.MESH
F32 = jnp.float32
BF16 = jnp.bfloat16
T = 1024
R = 128
H = 4
DH = 128
F = H * DH
D = 4096
B = 256
NB = T // B
NC = 8
CW = D // NC
SCALE = 1.0 / math.sqrt(DH)
NT = (((1,), (1,)), ((), ()))


def dot(a, b):
    return jnp.dot(a, b, preferred_element_type=F32)


def dot_nt(a, b):
    return lax.dot_general(a, b, NT, preferred_element_type=F32)


def mult(x, n):
    return pl.multiple_of(x, n)


def kernel(
    go, q, k, v, w, starts,
    dq_o, dk_o, dv_o, wg_o,
    qs, ks, vs, kT, vT, G, ow, PT, OT, bias, dOacc, dO, Wb, rx, rz, s1b, s2b, rx2, rz2, fin,
    dQT, dqs, dKa, dVa, dkb, dvb,
    s_q, r_q, s_k, r_k, s_v, r_v, l_q, l_k, l_v,
    s_ag, r_m, r_p, r_o, r_s, l_g, l_w,
    s_x, r_x, s_z, r_z, s_x2, r_x2, s_z2, r_z2,
    s_dq, r_dq, s_dk, r_dk, s_dv, r_dv, l_dq, l_dk, l_dv,
):
    dp = lax.axis_index("dp")
    me = lax.axis_index("seq")
    X, Z = dp // 4, lax.rem(dp, 4)
    Y, C = me // 2, lax.rem(me, 2)
    par = lax.rem(Z, 2)

    def seq_dev(s):
        return (dp, s)

    def grid_dev(x, z):
        return (x * 4 + z, me)

    def remote(src, dst, ss, rs, dev):
        return pltpu.make_async_remote_copy(
            src_ref=src, dst_ref=dst, send_sem=ss, recv_sem=rs, device_id=dev, device_id_type=MESH
        )

    up = seq_dev(lax.rem(Y + 1, 4) * 2 + C)
    down = seq_dev(lax.rem(Y + 3, 4) * 2 + C)
    sib = seq_dev(Y * 2 + 1 - C)

    barrier = pltpu.get_barrier_semaphore()
    for o in range(1, 8):
        pl.semaphore_signal(
            barrier, 1, device_id=seq_dev(lax.rem(me + o, 8)), device_id_type=MESH
        )
    for o in range(1, 4):
        pl.semaphore_signal(
            barrier, 1, device_id=grid_dev(lax.rem(X + o, 4), Z), device_id_type=MESH
        )
        pl.semaphore_signal(
            barrier, 1, device_id=grid_dev(X, lax.rem(Z + o, 4)), device_id_type=MESH
        )
    pl.semaphore_wait(barrier, 13)

    my_rows = pl.ds(mult(me * R, R), R)

    for o in (4, 5, 3, 2, 6, 1, 7):
        g = lax.rem(me + o, 8)
        remote(k.at[:, pl.ds(mult(g * DH, DH), DH)], ks.at[my_rows], s_k, r_k, seq_dev(g)).start()
        remote(v.at[:, pl.ds(mult(g * DH, DH), DH)], vs.at[my_rows], s_v, r_v, seq_dev(g)).start()
        remote(q.at[:, pl.ds(mult(g * F, F), F)], qs.at[my_rows], s_q, r_q, seq_dev(g)).start()
    own_q = pltpu.make_async_copy(q.at[:, pl.ds(mult(me * F, F), F)], qs.at[my_rows], l_q)
    own_k = pltpu.make_async_copy(k.at[:, pl.ds(mult(me * DH, DH), DH)], ks.at[my_rows], l_k)
    own_v = pltpu.make_async_copy(v.at[:, pl.ds(mult(me * DH, DH), DH)], vs.at[my_rows], l_v)
    own_q.start()
    own_k.start()
    own_v.start()

    def chunk_cols(j):
        xb = lax.rem(X + 1 + j // 2, 4)
        zp = lax.rem(Z // 2 + 1 + lax.rem(j, 2), 2)
        return pl.ds(mult((xb * 2 + zp) * CW, CW), CW)

    def rows_of(s):
        return pl.ds(mult(s * R, R), R)

    def send_own(j):
        src = go.at[:, chunk_cols(j)]
        dst = G.at[j, my_rows]
        remote(src, dst, s_ag, r_p.at[j], up).start()
        remote(src, dst, s_ag, r_m.at[j], down).start()
        remote(src, dst, s_ag, r_s.at[j], sib).start()

    from_down = lax.rem(Y + 3, 4) * 2 + C
    from_up = lax.rem(Y + 1, 4) * 2 + C
    from_opp = lax.rem(Y + 2, 4) * 2 + C

    def piece(j, s):
        return G.at[j, rows_of(s)]

    def arrived(j, s, sem):
        pltpu.make_async_copy(piece(j, s), piece(j, s), sem).wait()

    def relay(j, upward):
        lo, hi = piece(j, from_down), piece(j, from_up)
        if upward:
            arrived(j, from_down, r_p.at[j])
            remote(lo, lo, s_ag, r_o.at[j], up).start()
            arrived(j, from_up, r_m.at[j])
        else:
            arrived(j, from_up, r_m.at[j])
            remote(hi, hi, s_ag, r_o.at[j], down).start()
            arrived(j, from_down, r_p.at[j])
        remote(lo, lo, s_ag, r_s.at[j], sib).start()
        remote(hi, hi, s_ag, r_s.at[j], sib).start()

    for j in range(NC):
        pltpu.make_async_copy(go.at[:, chunk_cols(j)], G.at[j, my_rows], l_g).start()
        pltpu.make_async_copy(w.at[:, chunk_cols(j)], ow.at[j], l_w).start()
    for j in range(4):
        send_own(j)

    for i in range(NB):
        t = i * B + lax.broadcasted_iota(jnp.int32, (1, B), 1)
        opening = jnp.zeros((1, B), jnp.int32)
        for d in range(8):
            s = starts[0, d]
            opening = jnp.maximum(opening, jnp.where(s <= t, s, 0))
        n = (i + 1) * B
        u = lax.broadcasted_iota(jnp.int32, (n, B), 0)
        bias[i, :n] = jnp.where((u >= opening) & (u <= t), 0.0, -1e30)

    own_q.wait()
    own_k.wait()
    own_v.wait()
    pltpu.make_async_copy(ks.at[pl.ds(0, 7 * R)], ks.at[pl.ds(0, 7 * R)], r_k).wait()
    pltpu.make_async_copy(vs.at[pl.ds(0, 7 * R)], vs.at[pl.ds(0, 7 * R)], r_v).wait()
    for i in range(NB):
        kT[i] = ks[pl.ds(i * B, B)].T
    vT[...] = vs[...].T
    pltpu.make_async_copy(qs.at[pl.ds(0, 7 * R)], qs.at[pl.ds(0, 7 * R)], r_q).wait()

    def forward(h, upward):
        cols = pl.ds(mult(h * DH, DH), DH)
        for i in range(NB):
            n = (i + 1) * B
            st = dot_nt(ks[:n], qs[pl.ds(i * B, B), cols])
            st = st * (SCALE * math.log2(math.e)) + bias[i, :n]
            top = jnp.max(st, axis=0, keepdims=True)
            p = jnp.exp2(st - top)
            p = (p * (1.0 / jnp.sum(p, axis=0, keepdims=True))).astype(BF16)
            PT[h, i, :n] = p
            OT[cols, pl.ds(i * B, B)] = dot(vT[:, :n], p).astype(BF16)
        relay(h, upward)
        send_own(h + 4)

    def forward_pair(g, _):
        forward(2 * g, True)
        forward(2 * g + 1, False)
        return 0

    lax.fori_loop(0, H // 2, forward_pair, 0)

    pltpu.make_async_copy(G.at[0], G.at[0], l_g).wait()
    pltpu.make_async_copy(ow, ow, l_w).wait()

    def gathered(j):
        arrived(j, from_opp, r_o.at[j])
        opp = piece(j, from_opp)
        remote(opp, opp, s_ag, r_s.at[j], sib).start()
        half = G.at[j, pl.ds(0, 4 * R)]
        pltpu.make_async_copy(half, half, r_s.at[j]).wait()

    def dense(j):
        part = dot_nt(G[j], ow[j])

        @pl.when(j == 0)
        def _():
            dOacc[...] = part

        @pl.when(j > 0)
        def _():
            dOacc[...] += part

        Wb[j] = dot(OT[...], G[j]).astype(BF16)

    def chunk_pair(g, _):
        other = 1 - Z // 2
        for e in range(2):
            j = 2 * g + e
            gathered(j)
            dense(j)

            @pl.when(g < 2)
            def _():
                relay(j + 4, e == 0)

            @pl.when(g < 3)
            def _():
                remote(
                    Wb.at[j, pl.ds(0, 256)], rx.at[g, e], s_x, r_x,
                    grid_dev(lax.rem(X + 1 + g, 4), Z),
                ).start()

            if e == 0:
                for c in range(2):
                    zz = 2 * other + c
                    slot = lax.rem(zz - Z + 4, 4) - 1
                    remote(
                        Wb.at[j, pl.ds(256, 256), pl.ds(c * 256, 256)], rz.at[slot, g], s_z, r_z,
                        grid_dev(X, zz),
                    ).start()
            else:
                zz = Z + 1 - 2 * par
                slot = lax.rem(zz - Z + 4, 4) - 1
                remote(
                    Wb.at[j, pl.ds(256, 256), pl.ds(mult((1 - par) * 256, 256), 256)],
                    rz.at[slot, g], s_z, r_z, grid_dev(X, zz),
                ).start()
        return 0

    lax.fori_loop(0, NC // 2, chunk_pair, 0)
    dO[...] = dOacc[...].astype(BF16)
    dKa[...] = jnp.zeros_like(dKa)
    dVa[...] = jnp.zeros_like(dVa)

    def backward(b):
        rows = pl.ds(mult(b * B, B), B)
        hc = [pl.ds(h * DH, DH) for h in range(H)]
        deltas = []
        for h in range(H):
            gT = dO[rows, hc[h]].astype(F32).T
            deltas.append(jnp.sum(gT * OT[hc[h], rows].astype(F32), axis=0, keepdims=True))
        dQT[...] = jnp.zeros_like(dQT)

        def block(kb, _):
            keys = pl.ds(mult(kb * B, B), B)
            kk, vv = kT[kb], vs[keys]
            dk = jnp.zeros((B, DH), F32)
            dv = jnp.zeros((B, DH), F32)
            for h in range(H):
                p = PT[h, b, keys]
                g = dO[rows, hc[h]]
                dp_ = dot_nt(vv, g)
                ds = (p.astype(F32) * (dp_ - deltas[h])).astype(BF16)
                dv += dot(p, g)
                dk += dot(ds, qs[rows, hc[h]])
                dQT[h] += dot(kk, ds)
            dKa[keys] += dk
            dVa[keys] += dv
            return 0

        lax.fori_loop(0, b + 1, block, 0)
        for h in range(H):
            dqs[b, :, hc[h]] = (dQT[h].T * SCALE).astype(BF16)

    my_f = pl.ds(mult(me * F, F), F)
    my_d = pl.ds(mult(me * DH, DH), DH)

    def far_block(step, _):
        b = lax.rem(Y + 1 + step, 4)
        backward(b)
        for c in range(2):
            remote(
                dqs.at[b, pl.ds(c * R, R)], dq_o.at[:, my_f], s_dq, r_dq, seq_dev(b * 2 + c)
            ).start()
        return 0

    lax.fori_loop(0, 3, far_block, 0)
    backward(Y)
    other_rows = pl.ds(mult((1 - C) * R, R), R)
    own_rows = pl.ds(mult(C * R, R), R)
    remote(dqs.at[Y, other_rows], dq_o.at[:, my_f], s_dq, r_dq, sib).start()
    own_dq = pltpu.make_async_copy(dqs.at[Y, own_rows], dq_o.at[:, my_f], l_dq)
    own_dq.start()

    dkb[...] = (dKa[...] * SCALE).astype(BF16)
    dvb[...] = dVa[...].astype(BF16)
    for o in (4, 5, 3, 2, 6, 1, 7):
        g = lax.rem(me + o, 8)
        remote(dkb.at[rows_of(g)], dk_o.at[:, my_d], s_dk, r_dk, seq_dev(g)).start()
        remote(dvb.at[rows_of(g)], dv_o.at[:, my_d], s_dv, r_dv, seq_dev(g)).start()
    own_dk = pltpu.make_async_copy(dkb.at[my_rows], dk_o.at[:, my_d], l_dk)
    own_dv = pltpu.make_async_copy(dvb.at[my_rows], dv_o.at[:, my_d], l_dv)
    own_dk.start()
    own_dv.start()

    pltpu.make_async_copy(rx, rx, r_x).wait()
    for e in range(2):
        s = Wb[6 + e, :256].astype(F32)
        for i in range(3):
            s += rx[i, e].astype(F32)
        s1b[e] = s.astype(BF16)
    other = 1 - Z // 2
    for c in range(2):
        zz = 2 * other + c
        slot = lax.rem(zz - Z + 4, 4) - 1
        remote(
            s1b.at[0, :, pl.ds(c * 256, 256)], rx2.at[slot], s_x2, r_x2, grid_dev(X, zz)
        ).start()
    zz = Z + 1 - 2 * par
    slot = lax.rem(zz - Z + 4, 4) - 1
    remote(
        s1b.at[1, :, pl.ds(mult((1 - par) * 256, 256), 256)], rx2.at[slot], s_x2, r_x2,
        grid_dev(X, zz),
    ).start()

    pltpu.make_async_copy(rz, rz, r_z).wait()
    own_cols = pl.ds(mult(par * 256, 256), 256)
    for g in range(4):
        s = Wb[2 * g + 1, 256:, own_cols].astype(F32)
        for i in range(3):
            s += rz[i, g].astype(F32)
        if g < 3:
            s2b[g] = s.astype(BF16)
            remote(
                s2b.at[g], rz2.at[g], s_z2, r_z2, grid_dev(lax.rem(X + 1 + g, 4), Z)
            ).start()
        else:
            fin[...] = s

    pltpu.make_async_copy(rx2, rx2, r_x2).wait()
    norm = 1.0 / math.sqrt(T * 16)
    s = s1b[1, :, own_cols].astype(F32)
    for i in range(3):
        s += rx2[i].astype(F32)
    wg_o[:256] = s * norm
    pltpu.make_async_copy(rz2, rz2, r_z2).wait()
    s = fin[...]
    for i in range(3):
        s += rz2[i].astype(F32)
    wg_o[256:] = s * norm

    def drain(ref, *sems):
        for sem in sems:
            pltpu.make_async_copy(ref, ref, sem).wait()

    own_dq.wait()
    own_dk.wait()
    own_dv.wait()
    drain(qs.at[pl.ds(0, 7 * R)], s_q, s_dq, r_dq)
    drain(ks.at[pl.ds(0, 7 * R)], s_k, s_v, s_dk, s_dv, r_dk, r_dv)
    drain(G.at[pl.ds(0, 7)], s_ag)
    drain(rx, s_x)
    drain(rz, s_z)
    drain(rx2, s_x2, s_z2)


def body(grad_out, queries, keys, values, out_weight, doc_starts):
    vm = pltpu.VMEM
    dma = pltpu.SemaphoreType.DMA
    hbm = pl.BlockSpec(memory_space=pl.ANY)
    scratch = [
        vm((T, F), BF16),
        vm((T, DH), BF16),
        vm((T, DH), BF16),
        vm((NB, DH, B), BF16),
        vm((DH, T), BF16),
        vm((NC, T, CW), BF16),
        vm((NC, F, CW), BF16),
        vm((H, NB, T, B), BF16),
        vm((F, T), BF16),
        vm((NB, T, B), F32),
        vm((T, F), F32),
        vm((T, F), BF16),
        vm((NC, F, CW), BF16),
        vm((3, 2, 256, 512), BF16),
        vm((3, 4, 256, 256), BF16),
        vm((2, 256, 512), BF16),
        vm((3, 256, 256), BF16),
        vm((3, 256, 256), BF16),
        vm((3, 256, 256), BF16),
        vm((256, 256), F32),
        vm((H, DH, B), F32),
        vm((NB, B, F), BF16),
        vm((T, DH), F32),
        vm((T, DH), F32),
        vm((T, DH), BF16),
        vm((T, DH), BF16),
    ]
    scratch += [dma] * 9
    scratch += [dma, dma((NC,)), dma((NC,)), dma((NC,)), dma((NC,)), dma, dma]
    scratch += [dma] * 8
    scratch += [dma] * 9
    out = pl.pallas_call(
        kernel,
        name="attention_back",
        out_shape=(
            jax.ShapeDtypeStruct((R, D), BF16),
            jax.ShapeDtypeStruct((R, 1024), BF16),
            jax.ShapeDtypeStruct((R, 1024), BF16),
            jax.ShapeDtypeStruct((F, 256), F32),
        ),
        in_specs=[hbm] * 5 + [pl.BlockSpec(memory_space=pltpu.SMEM)],
        out_specs=(hbm, hbm, hbm, pl.BlockSpec(memory_space=pltpu.VMEM)),
        scratch_shapes=scratch,
        compiler_params=pltpu.CompilerParams(
            collective_id=0, has_side_effects=True, vmem_limit_bytes=60 * 1024 * 1024
        ),
    )(grad_out[0], queries[0], keys[0], values[0], out_weight, doc_starts)
    return (out[0][None], out[1][None], out[2][None], out[3])


def solution(mesh):
    return jax.shard_map(
        body,
        mesh=mesh,
        in_specs=(
            P("dp", "seq", None),
            P("dp", "seq", None),
            P("dp", "seq", None),
            P("dp", "seq", None),
            P("seq", None),
            P("dp", None),
        ),
        out_specs=(
            P("dp", "seq", None),
            P("dp", "seq", None),
            P("dp", "seq", None),
            P("seq", "dp"),
        ),
        check_vma=False,
    )
```

```python
import math

import jax
import jax.numpy as jnp
from jax import lax
from jax.experimental import pallas as pl
from jax.experimental.pallas import tpu as pltpu
from jax.sharding import PartitionSpec as P

MESH = pl.DeviceIdType.MESH
F32 = jnp.float32
BF16 = jnp.bfloat16
T = 1024
R = 128
H = 4
DH = 128
F = H * DH
D = 4096
B = 256
NB = T // B
NC = 8
CW = D // NC
CHUNK_X = (2, 2, 1, 3, 1, 3, 0, 0)
EARLY = 2
CHUNK_OWN = (0, 1, 0, 0, 1, 1, 0, 1)
SCALE = 1.0 / math.sqrt(DH)
NT = (((1,), (1,)), ((), ()))


def dot(a, b):
    return jnp.dot(a, b, preferred_element_type=F32)


def dot_nt(a, b):
    return lax.dot_general(a, b, NT, preferred_element_type=F32)


def mult(x, n):
    return pl.multiple_of(x, n)


def kernel(
    go, q, k, v, w, starts,
    dq_o, dk_o, dv_o, wg_o,
    qs, ks, vs, kT, vT, G, ow, PT, OT, bias, dOacc, dO, Wacc, Wb, rx, rz, s1b, s2b, rx2, rz2, fin,
    dqs, dKa, dVa, dkb, dvb,
    s_q, r_q, s_k, r_k, s_v, r_v, l_q, l_k, l_v,
    s_ag, r_m, r_p, r_o, r_own, r_near, r_opp, l_g, l_w,
    s_x, r_x, s_z, s_x2, r_x2, s_z2, r_z2, r_z,
    s_dq, r_dq, s_dk, r_dk, s_dv, r_dv, l_dq, l_dk, l_dv,
):
    dp = lax.axis_index("dp")
    me = lax.axis_index("seq")
    X, Z = dp // 4, lax.rem(dp, 4)
    Y, C = me // 2, lax.rem(me, 2)
    par = lax.rem(Z, 2)

    def seq_dev(s):
        return (dp, s)

    def grid_dev(x, z):
        return (x * 4 + z, me)

    def remote(src, dst, ss, rs, dev):
        return pltpu.make_async_remote_copy(
            src_ref=src, dst_ref=dst, send_sem=ss, recv_sem=rs, device_id=dev, device_id_type=MESH
        )

    up = seq_dev(lax.rem(Y + 1, 4) * 2 + C)
    down = seq_dev(lax.rem(Y + 3, 4) * 2 + C)
    sib = seq_dev(Y * 2 + 1 - C)

    barrier = pltpu.get_barrier_semaphore()
    for o in range(1, 8):
        pl.semaphore_signal(
            barrier, 1, device_id=seq_dev(lax.rem(me + o, 8)), device_id_type=MESH
        )
    for o in range(1, 4):
        pl.semaphore_signal(
            barrier, 1, device_id=grid_dev(lax.rem(X + o, 4), Z), device_id_type=MESH
        )
        pl.semaphore_signal(
            barrier, 1, device_id=grid_dev(X, lax.rem(Z + o, 4)), device_id_type=MESH
        )
    pl.semaphore_wait(barrier, 13)

    my_rows = pl.ds(mult(me * R, R), R)

    for o in (4, 5, 3, 2, 6, 1, 7):
        g = lax.rem(me + o, 8)
        remote(k.at[:, pl.ds(mult(g * DH, DH), DH)], ks.at[my_rows], s_k, r_k, seq_dev(g)).start()
        remote(v.at[:, pl.ds(mult(g * DH, DH), DH)], vs.at[my_rows], s_v, r_v, seq_dev(g)).start()
        remote(q.at[:, pl.ds(mult(g * F, F), F)], qs.at[my_rows], s_q, r_q, seq_dev(g)).start()
    own_q = pltpu.make_async_copy(q.at[:, pl.ds(mult(me * F, F), F)], qs.at[my_rows], l_q)
    own_k = pltpu.make_async_copy(k.at[:, pl.ds(mult(me * DH, DH), DH)], ks.at[my_rows], l_k)
    own_v = pltpu.make_async_copy(v.at[:, pl.ds(mult(me * DH, DH), DH)], vs.at[my_rows], l_v)
    own_q.start()
    own_k.start()
    own_v.start()

    def chunk_cols(j):
        xb = lax.rem(X + CHUNK_X[j], 4)
        zp = Z // 2 if CHUNK_OWN[j] else 1 - Z // 2
        return pl.ds(mult((xb * 2 + zp) * CW, CW), CW)

    def rows_of(s):
        return pl.ds(mult(s * R, R), R)

    def block_of(b):
        return pl.ds(mult(b * B, B), B)

    def send_own(j):
        src = go.at[:, chunk_cols(j)]
        dst = G.at[j, my_rows]
        remote(src, dst, s_ag, r_p.at[j], up).start()
        remote(src, dst, s_ag, r_m.at[j], down).start()

    y_up, y_down, y_opp = lax.rem(Y + 1, 4), lax.rem(Y + 3, 4), lax.rem(Y + 2, 4)
    from_down, from_up, from_opp = y_down * 2 + C, y_up * 2 + C, y_opp * 2 + C

    def piece(j, s):
        return G.at[j, rows_of(s)]

    def arrived(j, s, sem):
        pltpu.make_async_copy(piece(j, s), piece(j, s), sem).wait()

    def relay(j):
        lo, hi = piece(j, from_down), piece(j, from_up)
        if j % 2 == 0:
            arrived(j, from_down, r_p.at[j])
            remote(lo, lo, s_ag, r_o.at[j], up).start()
            arrived(j, from_up, r_m.at[j])
        else:
            arrived(j, from_up, r_m.at[j])
            remote(hi, hi, s_ag, r_o.at[j], down).start()
            arrived(j, from_down, r_p.at[j])
        remote(lo, lo, s_ag, r_near.at[j], sib).start()
        remote(hi, hi, s_ag, r_near.at[j], sib).start()

    for j in range(NC):
        pltpu.make_async_copy(go.at[:, chunk_cols(j)], G.at[j, my_rows], l_g).start()
        pltpu.make_async_copy(w.at[:, chunk_cols(j)], ow.at[j], l_w).start()
    for j in range(4):
        send_own(j)
    for j in range(NC):
        remote(go.at[:, chunk_cols(j)], G.at[j, my_rows], s_ag, r_own.at[j], sib).start()

    for i in range(NB):
        t = i * B + lax.broadcasted_iota(jnp.int32, (1, B), 1)
        opening = jnp.zeros((1, B), jnp.int32)
        for d in range(8):
            s = starts[0, d]
            opening = jnp.maximum(opening, jnp.where(s <= t, s, 0))
        n = (i + 1) * B
        u = lax.broadcasted_iota(jnp.int32, (n, B), 0)
        bias[i, :n] = jnp.where((u >= opening) & (u <= t), 0.0, -1e30)
    dKa[...] = jnp.zeros_like(dKa)
    dVa[...] = jnp.zeros_like(dVa)

    pltpu.make_async_copy(G.at[0], G.at[0], l_g).wait()
    pltpu.make_async_copy(ow, ow, l_w).wait()

    def project(j, b, first):
        rows = block_of(b)
        part = dot_nt(G[j, rows], ow[j])
        dOacc[rows] = part if first else dOacc[rows] + part

    def projected(b):
        rows = block_of(b)
        dO[rows] = dOacc[rows].astype(BF16)

    for j in range(NC):
        arrived(j, me + 1 - 2 * C, r_own.at[j])
        project(j, Y, j == 0)
    projected(Y)

    own_q.wait()
    own_k.wait()
    own_v.wait()
    pltpu.make_async_copy(ks.at[pl.ds(0, 7 * R)], ks.at[pl.ds(0, 7 * R)], r_k).wait()
    pltpu.make_async_copy(vs.at[pl.ds(0, 7 * R)], vs.at[pl.ds(0, 7 * R)], r_v).wait()
    kT[...] = ks[...].T
    vT[...] = vs[...].T
    pltpu.make_async_copy(qs.at[pl.ds(0, 7 * R)], qs.at[pl.ds(0, 7 * R)], r_q).wait()

    for h in range(H):
        cols = pl.ds(h * DH, DH)
        for i in range(NB):
            n = (i + 1) * B
            st = dot_nt(ks[:n], qs[pl.ds(i * B, B), cols])
            st = st * (SCALE * math.log2(math.e)) + bias[i, :n]
            top = jnp.max(st, axis=0, keepdims=True)
            p = jnp.exp2(st - top)
            p = (p * (1.0 / jnp.sum(p, axis=0, keepdims=True))).astype(BF16)
            PT[h, i, :n] = p
            OT[cols, pl.ds(i * B, B)] = dot(vT[:, :n], p).astype(BF16)
        if h < EARLY:
            relay(h)
        send_own(h + 4)

    hc = [pl.ds(h * DH, DH) for h in range(H)]

    def backward(b):
        rows = block_of(b)

        def pair(n, g):
            cols = [pl.ds(mult((2 * g + e) * DH, DH), DH) for e in range(2)]
            ps, gs, dss = [], [], []
            for e in range(2):
                grad = dO[rows, cols[e]]
                gT = grad.astype(F32).T
                delta = jnp.sum(gT * OT[cols[e], rows].astype(F32), axis=0, keepdims=True)
                p = PT[2 * g + e, b, :n]
                ds = (p.astype(F32) * (dot_nt(vs[:n], grad) - delta)).astype(BF16)
                dqs[b, :, cols[e]] = (dot(kT[:, :n], ds).T * SCALE).astype(BF16)
                ps.append(p)
                gs.append(grad)
                dss.append(ds)
            dVa[:n] += dot(jnp.concatenate(ps, axis=1), jnp.concatenate(gs, axis=0))
            qq = jnp.concatenate([qs[rows, c] for c in cols], axis=0)
            dKa[:n] += dot(jnp.concatenate(dss, axis=1), qq)

        for i in range(NB):

            @pl.when(b == i)
            def _():
                @pl.loop(0, H // 2)
                def _(g):
                    pair((i + 1) * B, g)

    my_f = pl.ds(mult(me * F, F), F)
    my_d = pl.ds(mult(me * DH, DH), DH)

    def send_dq(b):
        for c in range(2):
            remote(
                dqs.at[b, pl.ds(c * R, R)], dq_o.at[:, my_f], s_dq, r_dq, seq_dev(b * 2 + c)
            ).start()

    backward(Y)
    other_rows = pl.ds(mult((1 - C) * R, R), R)
    own_rows = pl.ds(mult(C * R, R), R)
    remote(dqs.at[Y, other_rows], dq_o.at[:, my_f], s_dq, r_dq, sib).start()
    own_dq = pltpu.make_async_copy(dqs.at[Y, own_rows], dq_o.at[:, my_f], l_dq)
    own_dq.start()

    def opposite(j):
        arrived(j, from_opp, r_o.at[j])
        opp = piece(j, from_opp)
        remote(opp, opp, s_ag, r_opp.at[j], sib).start()

    def near_here(j):
        half = G.at[j, pl.ds(0, 2 * R)]
        pltpu.make_async_copy(half, half, r_near.at[j]).wait()

    other = 1 - Z // 2

    def z_slot(zz):
        return lax.rem(zz - Z + 4, 4) - 1

    def scatter(j):
        dx = CHUNK_X[j]
        if dx:
            remote(
                Wb.at[j, pl.ds(0, 256)], rx.at[dx - 1, CHUNK_OWN[j]], s_x, r_x,
                grid_dev(lax.rem(X + dx, 4), Z),
            ).start()
        if CHUNK_OWN[j]:
            sends = [(mult((1 - par) * 256, 256), Z + 1 - 2 * par)]
        else:
            sends = [(c * 256, 2 * other + c) for c in range(2)]
        for col, zz in sends:
            remote(
                Wb.at[j, pl.ds(256, 256), pl.ds(col, 256)], rz.at[dx, z_slot(zz)], s_z, r_z.at[dx],
                grid_dev(X, zz),
            ).start()

    def near(j):
        near_here(j)
        s = None
        for b in (Y, y_up, y_down):
            d = dot(OT[:, block_of(b)], G[j, block_of(b)])
            s = d if s is None else s + d
        Wacc[j - 2] = s
        for b in (y_up, y_down):
            project(j, b, False)

    def full(j):
        arrived(j, y_opp * 2 + 1 - C, r_opp.at[j])
        near_here(j)
        for b in (y_up, y_down, y_opp):
            project(j, b, j == 0)
        Wb[j] = dot(OT[...], G[j]).astype(BF16)
        scatter(j)

    def finish(j):
        arrived(j, y_opp * 2 + 1 - C, r_opp.at[j])
        project(j, y_opp, False)
        Wb[j] = (Wacc[j - 2] + dot(OT[:, block_of(y_opp)], G[j, block_of(y_opp)])).astype(BF16)
        scatter(j)

    relay(2)
    relay(3)
    opposite(0)
    full(0)
    opposite(1)
    relay(4)
    near(2)
    full(1)
    relay(5)
    near(3)
    near(4)
    relay(6)
    near(5)
    relay(7)
    near(6)
    near(7)
    projected(y_up)
    projected(y_down)
    opposite(2)
    opposite(3)
    backward(y_up)
    send_dq(y_up)
    finish(2)
    finish(3)
    opposite(4)
    opposite(5)
    backward(y_down)
    send_dq(y_down)
    opposite(6)
    opposite(7)
    for j in range(4, NC):
        finish(j)
    projected(y_opp)
    backward(y_opp)
    send_dq(y_opp)

    dkb[...] = (dKa[...] * SCALE).astype(BF16)
    dvb[...] = dVa[...].astype(BF16)
    for o in (4, 5, 3, 2, 6, 1, 7):
        g = lax.rem(me + o, 8)
        remote(dkb.at[rows_of(g)], dk_o.at[:, my_d], s_dk, r_dk, seq_dev(g)).start()
        remote(dvb.at[rows_of(g)], dv_o.at[:, my_d], s_dv, r_dv, seq_dev(g)).start()
    own_dk = pltpu.make_async_copy(dkb.at[my_rows], dk_o.at[:, my_d], l_dk)
    own_dv = pltpu.make_async_copy(dvb.at[my_rows], dv_o.at[:, my_d], l_dv)
    own_dk.start()
    own_dv.start()

    chunk_at = {(CHUNK_X[j], CHUNK_OWN[j]): j for j in range(NC)}
    own_cols = pl.ds(mult(par * 256, 256), 256)

    def z_sum(dx):
        pltpu.make_async_copy(rz.at[dx], rz.at[dx], r_z.at[dx]).wait()
        s = Wb[chunk_at[dx, 1], 256:, own_cols].astype(F32)
        for i in range(3):
            s += rz[dx, i].astype(F32)
        if dx:
            s2b[dx - 1] = s.astype(BF16)
            remote(
                s2b.at[dx - 1], rz2.at[dx - 1], s_z2, r_z2, grid_dev(lax.rem(X + dx, 4), Z)
            ).start()
        else:
            fin[...] = s

    z_sum(2)
    z_sum(1)
    z_sum(3)
    pltpu.make_async_copy(rx, rx, r_x).wait()
    for e in range(2):
        s = Wb[chunk_at[0, e], :256].astype(F32)
        for i in range(3):
            s += rx[i, e].astype(F32)
        s1b[e] = s.astype(BF16)
    x_sends = [(0, c * 256, 2 * other + c) for c in range(2)]
    x_sends.append((1, mult((1 - par) * 256, 256), Z + 1 - 2 * par))
    for e, col, zz in x_sends:
        remote(
            s1b.at[e, :, pl.ds(col, 256)], rx2.at[z_slot(zz)], s_x2, r_x2, grid_dev(X, zz)
        ).start()

    z_sum(0)
    pltpu.make_async_copy(rx2, rx2, r_x2).wait()
    norm = 1.0 / math.sqrt(T * 16)
    s = s1b[1, :, own_cols].astype(F32)
    for i in range(3):
        s += rx2[i].astype(F32)
    wg_o[:256] = s * norm
    pltpu.make_async_copy(rz2, rz2, r_z2).wait()
    s = fin[...]
    for i in range(3):
        s += rz2[i].astype(F32)
    wg_o[256:] = s * norm

    def drain(ref, *sems):
        for sem in sems:
            pltpu.make_async_copy(ref, ref, sem).wait()

    own_dq.wait()
    own_dk.wait()
    own_dv.wait()
    drain(qs.at[pl.ds(0, 7 * R)], s_q, s_dq, r_dq)
    drain(ks.at[pl.ds(0, 7 * R)], s_k, s_v, s_dk, s_dv, r_dk, r_dv)
    drain(G.at[pl.ds(0, 7)], s_ag)
    drain(rx, s_x)
    drain(rz, s_z)
    drain(rx2, s_x2, s_z2)


def write_out(a, b, c, d, ao, bo, co, do, sem):
    copies = [
        pltpu.make_async_copy(src, dst, sem.at[i])
        for i, (src, dst) in enumerate(((a, ao), (b, bo), (c, co), (d, do)))
    ]
    for copy in copies:
        copy.start()
    for copy in copies:
        copy.wait()


def body(grad_out, queries, keys, values, out_weight, doc_starts):
    vm = pltpu.VMEM
    dma = pltpu.SemaphoreType.DMA
    hbm = pl.BlockSpec(memory_space=pl.ANY)
    scratch = [
        vm((T, F), BF16),
        vm((T, DH), BF16),
        vm((T, DH), BF16),
        vm((DH, T), BF16),
        vm((DH, T), BF16),
        vm((NC, T, CW), BF16),
        vm((NC, F, CW), BF16),
        vm((H, NB, T, B), BF16),
        vm((F, T), BF16),
        vm((NB, T, B), F32),
        vm((T, F), F32),
        vm((T, F), BF16),
        vm((NC - 2, F, CW), F32),
        vm((NC, F, CW), BF16),
        vm((3, 2, 256, 512), BF16),
        vm((4, 3, 256, 256), BF16),
        vm((2, 256, 512), BF16),
        vm((3, 256, 256), BF16),
        vm((3, 256, 256), BF16),
        vm((3, 256, 256), BF16),
        vm((256, 256), F32),
        vm((NB, B, F), BF16),
        vm((T, DH), F32),
        vm((T, DH), F32),
        vm((T, DH), BF16),
        vm((T, DH), BF16),
    ]
    scratch += [dma] * 9
    scratch += [dma] + [dma((NC,))] * 6 + [dma] * 2
    scratch += [dma] * 7 + [dma((4,))]
    scratch += [dma] * 9
    shapes = (((R, D), BF16), ((R, 1024), BF16), ((R, 1024), BF16), ((F, 256), F32))
    local = pl.BlockSpec(memory_space=pltpu.VMEM)
    held = pl.pallas_call(
        kernel,
        name="attention_back",
        out_shape=tuple(vm(shape, dtype) for shape, dtype in shapes),
        in_specs=[hbm] * 5 + [pl.BlockSpec(memory_space=pltpu.SMEM)],
        out_specs=(local,) * 4,
        scratch_shapes=scratch,
        compiler_params=pltpu.CompilerParams(
            collective_id=0, has_side_effects=True, vmem_limit_bytes=60 * 1024 * 1024
        ),
    )(grad_out[0], queries[0], keys[0], values[0], out_weight, doc_starts)
    out = pl.pallas_call(
        write_out,
        name="write_out",
        out_shape=tuple(jax.ShapeDtypeStruct(shape, dtype) for shape, dtype in shapes),
        in_specs=[local] * 4,
        out_specs=(hbm,) * 4,
        scratch_shapes=[dma((4,))],
    )(*[pltpu.with_memory_space_constraint(x, pltpu.VMEM) for x in held])
    return (out[0][None], out[1][None], out[2][None], out[3])


def solution(mesh):
    return jax.shard_map(
        body,
        mesh=mesh,
        in_specs=(
            P("dp", "seq", None),
            P("dp", "seq", None),
            P("dp", "seq", None),
            P("dp", "seq", None),
            P("seq", None),
            P("dp", None),
        ),
        out_specs=(
            P("dp", "seq", None),
            P("dp", "seq", None),
            P("dp", "seq", None),
            P("seq", "dp"),
        ),
        check_vma=False,
    )
```

```python
import math

import jax
import jax.numpy as jnp
from jax import lax
from jax.experimental import pallas as pl
from jax.experimental.pallas import tpu as pltpu
from jax.sharding import PartitionSpec as P

MESH = pl.DeviceIdType.MESH
F32 = jnp.float32
BF16 = jnp.bfloat16
T = 1024
R = 128
XR = 320
ZR = 512 - XR
H = 4
DH = 128
F = H * DH
D = 4096
B = 256
NB = T // B
NC = 8
CW = D // NC
CHUNK_X = (2, 2, 1, 3, 1, 3, 0, 0)
EARLY = 3
CHUNK_OWN = (0, 1, 0, 0, 1, 1, 0, 1)
SCALE = 1.0 / math.sqrt(DH)
NT = (((1,), (1,)), ((), ()))


def dot(a, b):
    return jnp.dot(a, b, preferred_element_type=F32)


def dot_nt(a, b):
    return lax.dot_general(a, b, NT, preferred_element_type=F32)


def mult(x, n):
    return pl.multiple_of(x, n)


def kernel(
    go, q, k, v, w, starts,
    dq_o, dk_o, dv_o, wg_o,
    qs, ks, vs, kT, vT, G, ow, PT, OT, bias, dOacc, dO, Wacc, Wb, rx, rz, s1b, s2b, rx2, rz2, fin,
    dqs, dKa, dVa, dkb, dvb,
    s_q, r_q, s_k, r_k, s_v, r_v, l_q, l_k, l_v,
    s_ag, r_m, r_p, r_o, r_own, r_near, r_opp, l_g, l_w,
    s_x, s_z, s_x2, r_x2, s_z2, r_z2, r_x, r_z,
    s_dq, r_dq, s_dk, r_dk, s_dv, r_dv, l_dq, l_dk, l_dv,
):
    dp = lax.axis_index("dp")
    me = lax.axis_index("seq")
    X, Z = dp // 4, lax.rem(dp, 4)
    Y, C = me // 2, lax.rem(me, 2)
    par = lax.rem(Z, 2)

    def seq_dev(s):
        return (dp, s)

    def grid_dev(x, z):
        return (x * 4 + z, me)

    def remote(src, dst, ss, rs, dev):
        return pltpu.make_async_remote_copy(
            src_ref=src, dst_ref=dst, send_sem=ss, recv_sem=rs, device_id=dev, device_id_type=MESH
        )

    up = seq_dev(lax.rem(Y + 1, 4) * 2 + C)
    down = seq_dev(lax.rem(Y + 3, 4) * 2 + C)
    sib = seq_dev(Y * 2 + 1 - C)

    barrier = pltpu.get_barrier_semaphore()
    for o in range(1, 8):
        pl.semaphore_signal(
            barrier, 1, device_id=seq_dev(lax.rem(me + o, 8)), device_id_type=MESH
        )
    for o in range(1, 4):
        pl.semaphore_signal(
            barrier, 1, device_id=grid_dev(lax.rem(X + o, 4), Z), device_id_type=MESH
        )
        pl.semaphore_signal(
            barrier, 1, device_id=grid_dev(X, lax.rem(Z + o, 4)), device_id_type=MESH
        )
    pl.semaphore_wait(barrier, 13)

    my_rows = pl.ds(mult(me * R, R), R)

    for o in (4, 5, 3, 2, 6, 1, 7):
        g = lax.rem(me + o, 8)
        remote(k.at[:, pl.ds(mult(g * DH, DH), DH)], ks.at[my_rows], s_k, r_k, seq_dev(g)).start()
        remote(v.at[:, pl.ds(mult(g * DH, DH), DH)], vs.at[my_rows], s_v, r_v, seq_dev(g)).start()
        remote(q.at[:, pl.ds(mult(g * F, F), F)], qs.at[my_rows], s_q, r_q, seq_dev(g)).start()
    own_q = pltpu.make_async_copy(q.at[:, pl.ds(mult(me * F, F), F)], qs.at[my_rows], l_q)
    own_k = pltpu.make_async_copy(k.at[:, pl.ds(mult(me * DH, DH), DH)], ks.at[my_rows], l_k)
    own_v = pltpu.make_async_copy(v.at[:, pl.ds(mult(me * DH, DH), DH)], vs.at[my_rows], l_v)
    own_q.start()
    own_k.start()
    own_v.start()

    def chunk_cols(j):
        xb = lax.rem(X + CHUNK_X[j], 4)
        zp = Z // 2 if CHUNK_OWN[j] else 1 - Z // 2
        return pl.ds(mult((xb * 2 + zp) * CW, CW), CW)

    def rows_of(s):
        return pl.ds(mult(s * R, R), R)

    def block_of(b):
        return pl.ds(mult(b * B, B), B)

    def send_own(j):
        src = go.at[:, chunk_cols(j)]
        dst = G.at[j, my_rows]
        remote(src, dst, s_ag, r_p.at[j], up).start()
        remote(src, dst, s_ag, r_m.at[j], down).start()

    y_up, y_down, y_opp = lax.rem(Y + 1, 4), lax.rem(Y + 3, 4), lax.rem(Y + 2, 4)
    from_down, from_up, from_opp = y_down * 2 + C, y_up * 2 + C, y_opp * 2 + C

    def piece(j, s):
        return G.at[j, rows_of(s)]

    def arrived(j, s, sem):
        pltpu.make_async_copy(piece(j, s), piece(j, s), sem).wait()

    def relay(j):
        lo, hi = piece(j, from_down), piece(j, from_up)
        if j % 2 == 0:
            arrived(j, from_down, r_p.at[j])
            remote(lo, lo, s_ag, r_o.at[j], up).start()
            arrived(j, from_up, r_m.at[j])
        else:
            arrived(j, from_up, r_m.at[j])
            remote(hi, hi, s_ag, r_o.at[j], down).start()
            arrived(j, from_down, r_p.at[j])
        remote(lo, lo, s_ag, r_near.at[j], sib).start()
        remote(hi, hi, s_ag, r_near.at[j], sib).start()

    for j in range(NC):
        pltpu.make_async_copy(go.at[:, chunk_cols(j)], G.at[j, my_rows], l_g).start()
        pltpu.make_async_copy(w.at[:, chunk_cols(j)], ow.at[j], l_w).start()
    for j in range(4):
        send_own(j)
    for j in range(NC):
        remote(go.at[:, chunk_cols(j)], G.at[j, my_rows], s_ag, r_own.at[j], sib).start()

    for i in range(NB):
        t = i * B + lax.broadcasted_iota(jnp.int32, (1, B), 1)
        opening = jnp.zeros((1, B), jnp.int32)
        for d in range(8):
            s = starts[0, d]
            opening = jnp.maximum(opening, jnp.where(s <= t, s, 0))
        n = (i + 1) * B
        u = lax.broadcasted_iota(jnp.int32, (n, B), 0)
        bias[i, :n] = jnp.where((u >= opening) & (u <= t), 0.0, -1e30)
    dKa[...] = jnp.zeros_like(dKa)
    dVa[...] = jnp.zeros_like(dVa)

    pltpu.make_async_copy(G.at[0], G.at[0], l_g).wait()
    pltpu.make_async_copy(ow, ow, l_w).wait()

    def project(j, b, first):
        rows = block_of(b)
        part = dot_nt(G[j, rows], ow[j])
        dOacc[rows] = part if first else dOacc[rows] + part

    def projected(b):
        rows = block_of(b)
        dO[rows] = dOacc[rows].astype(BF16)

    for j in range(NC):
        arrived(j, me + 1 - 2 * C, r_own.at[j])
        project(j, Y, j == 0)
    projected(Y)

    own_q.wait()
    own_k.wait()
    own_v.wait()
    pltpu.make_async_copy(ks.at[pl.ds(0, 7 * R)], ks.at[pl.ds(0, 7 * R)], r_k).wait()
    pltpu.make_async_copy(vs.at[pl.ds(0, 7 * R)], vs.at[pl.ds(0, 7 * R)], r_v).wait()
    kT[...] = ks[...].T
    vT[...] = vs[...].T
    pltpu.make_async_copy(qs.at[pl.ds(0, 7 * R)], qs.at[pl.ds(0, 7 * R)], r_q).wait()

    for h in range(H):
        cols = pl.ds(h * DH, DH)
        for i in range(NB):
            n = (i + 1) * B
            st = dot_nt(ks[:n], qs[pl.ds(i * B, B), cols])
            st = st * (SCALE * math.log2(math.e)) + bias[i, :n]
            top = jnp.max(st, axis=0, keepdims=True)
            p = jnp.exp2(st - top)
            p = (p * (1.0 / jnp.sum(p, axis=0, keepdims=True))).astype(BF16)
            PT[h, i, :n] = p
            OT[cols, pl.ds(i * B, B)] = dot(vT[:, :n], p).astype(BF16)
        if h < EARLY:
            relay(h)
        send_own(h + 4)

    hc = [pl.ds(h * DH, DH) for h in range(H)]

    my_f = pl.ds(mult(me * F, F), F)
    my_d = pl.ds(mult(me * DH, DH), DH)

    def backward(b, far=True):
        rows = block_of(b)

        def pair(n, g):
            cols = [pl.ds(mult((2 * g + e) * DH, DH), DH) for e in range(2)]
            ps, gs, dss = [], [], []
            for e in range(2):
                grad = dO[rows, cols[e]]
                gT = grad.astype(F32).T
                delta = jnp.sum(gT * OT[cols[e], rows].astype(F32), axis=0, keepdims=True)
                p = PT[2 * g + e, b, :n]
                ds = (p.astype(F32) * (dot_nt(vs[:n], grad) - delta)).astype(BF16)
                dqs[b, :, cols[e]] = (dot(kT[:, :n], ds).T * SCALE).astype(BF16)
                ps.append(p)
                gs.append(grad)
                dss.append(ds)
            dVa[:n] += dot(jnp.concatenate(ps, axis=1), jnp.concatenate(gs, axis=0))
            for c in range(2 if far else 0):
                remote(
                    dqs.at[b, pl.ds(c * R, R), pl.ds(mult(g * B, B), B)],
                    dq_o.at[:, pl.ds(mult(me * F + g * B, B), B)],
                    s_dq, r_dq, seq_dev(b * 2 + c),
                ).start()
            qq = jnp.concatenate([qs[rows, c] for c in cols], axis=0)
            dKa[:n] += dot(jnp.concatenate(dss, axis=1), qq)

        for i in range(NB):

            @pl.when(b == i)
            def _():
                @pl.loop(0, H // 2)
                def _(g):
                    pair((i + 1) * B, g)

    backward(Y, False)
    other_rows = pl.ds(mult((1 - C) * R, R), R)
    own_rows = pl.ds(mult(C * R, R), R)
    remote(dqs.at[Y, other_rows], dq_o.at[:, my_f], s_dq, r_dq, sib).start()
    own_dq = pltpu.make_async_copy(dqs.at[Y, own_rows], dq_o.at[:, my_f], l_dq)
    own_dq.start()

    def opposite(j):
        arrived(j, from_opp, r_o.at[j])
        opp = piece(j, from_opp)
        remote(opp, opp, s_ag, r_opp.at[j], sib).start()

    def near_here(j):
        half = G.at[j, pl.ds(0, 2 * R)]
        pltpu.make_async_copy(half, half, r_near.at[j]).wait()

    other = 1 - Z // 2

    def z_slot(zz):
        return lax.rem(zz - Z + 4, 4) - 1

    def scatter(j):
        dx = CHUNK_X[j]
        if dx:
            remote(
                Wb.at[j, pl.ds(0, XR)], rx.at[CHUNK_OWN[j], dx - 1], s_x, r_x.at[CHUNK_OWN[j]],
                grid_dev(lax.rem(X + dx, 4), Z),
            ).start()
        if CHUNK_OWN[j]:
            sends = [(mult((1 - par) * 256, 256), Z + 1 - 2 * par)]
        else:
            sends = [(c * 256, 2 * other + c) for c in range(2)]
        for col, zz in sends:
            remote(
                Wb.at[j, pl.ds(XR, ZR), pl.ds(col, 256)], rz.at[dx, z_slot(zz)], s_z, r_z.at[dx],
                grid_dev(X, zz),
            ).start()

    def near(j):
        near_here(j)
        s = None
        for b in (Y, y_up, y_down):
            d = dot(OT[:, block_of(b)], G[j, block_of(b)])
            s = d if s is None else s + d
        Wacc[j - EARLY] = s
        for b in (y_up, y_down):
            project(j, b, False)

    def full(j):
        arrived(j, y_opp * 2 + 1 - C, r_opp.at[j])
        near_here(j)
        for b in (y_up, y_down, y_opp):
            project(j, b, j == 0)
        Wb[j] = dot(OT[...], G[j]).astype(BF16)
        scatter(j)

    def finish(j):
        arrived(j, y_opp * 2 + 1 - C, r_opp.at[j])
        project(j, y_opp, False)
        Wb[j] = (Wacc[j - EARLY] + dot(OT[:, block_of(y_opp)], G[j, block_of(y_opp)])).astype(BF16)
        scatter(j)

    relay(3)
    opposite(0)
    full(0)
    opposite(1)
    relay(4)
    near(3)
    full(1)
    relay(5)
    near(4)
    opposite(2)
    near(5)
    full(2)
    relay(6)
    near(6)
    relay(7)
    near(7)
    projected(y_up)
    projected(y_down)
    opposite(3)
    backward(y_up)
    finish(3)
    opposite(4)
    opposite(5)
    finish(4)
    finish(5)
    backward(y_down)
    opposite(6)
    opposite(7)
    finish(6)
    finish(7)
    projected(y_opp)

    def send_kv(kb):
        rows = pl.ds(kb * B, B)
        dkb[rows] = (dKa[rows] * SCALE).astype(BF16)
        dvb[rows] = dVa[rows].astype(BF16)
        for c in range(2):
            g = kb * 2 + c

            @pl.when(me != g)
            def _():
                remote(dkb.at[rows_of(g)], dk_o.at[:, my_d], s_dk, r_dk, seq_dev(g)).start()
                remote(dvb.at[rows_of(g)], dv_o.at[:, my_d], s_dv, r_dv, seq_dev(g)).start()

    for kb in range(1, NB):

        @pl.when((kb > y_opp) & (kb != Y))
        def _():
            send_kv(kb)

    backward(y_opp)
    for kb in range(NB):

        @pl.when((kb <= y_opp) | (kb == Y))
        def _():
            send_kv(kb)

    own_dk = pltpu.make_async_copy(dkb.at[my_rows], dk_o.at[:, my_d], l_dk)
    own_dv = pltpu.make_async_copy(dvb.at[my_rows], dv_o.at[:, my_d], l_dv)
    own_dk.start()
    own_dv.start()

    chunk_at = {(CHUNK_X[j], CHUNK_OWN[j]): j for j in range(NC)}
    own_cols = pl.ds(mult(par * 256, 256), 256)

    def z_sum(dx):
        pltpu.make_async_copy(rz.at[dx], rz.at[dx], r_z.at[dx]).wait()
        s = Wb[chunk_at[dx, 1], XR:, own_cols].astype(F32)
        for i in range(3):
            s += rz[dx, i].astype(F32)
        if dx:
            s2b[dx - 1] = s.astype(BF16)
            remote(
                s2b.at[dx - 1], rz2.at[dx - 1], s_z2, r_z2, grid_dev(lax.rem(X + dx, 4), Z)
            ).start()
        else:
            fin[...] = s

    def x_sum(e):
        pltpu.make_async_copy(rx.at[e], rx.at[e], r_x.at[e]).wait()
        s = Wb[chunk_at[0, e], :XR].astype(F32)
        for i in range(3):
            s += rx[e, i].astype(F32)
        s1b[e] = s.astype(BF16)
        if e:
            sends = [(mult((1 - par) * 256, 256), Z + 1 - 2 * par)]
        else:
            sends = [(c * 256, 2 * other + c) for c in range(2)]
        for col, zz in sends:
            remote(
                s1b.at[e, :, pl.ds(col, 256)], rx2.at[z_slot(zz)], s_x2, r_x2, grid_dev(X, zz)
            ).start()

    z_sum(2)
    x_sum(0)
    z_sum(1)
    z_sum(3)
    x_sum(1)
    z_sum(0)
    pltpu.make_async_copy(rx2, rx2, r_x2).wait()
    norm = 1.0 / math.sqrt(T * 16)
    s = s1b[1, :, own_cols].astype(F32)
    for i in range(3):
        s += rx2[i].astype(F32)
    wg_o[:XR] = s * norm
    pltpu.make_async_copy(rz2, rz2, r_z2).wait()
    s = fin[...]
    for i in range(3):
        s += rz2[i].astype(F32)
    wg_o[XR:] = s * norm

    def drain(ref, *sems):
        for sem in sems:
            pltpu.make_async_copy(ref, ref, sem).wait()

    own_dq.wait()
    own_dk.wait()
    own_dv.wait()
    drain(qs.at[pl.ds(0, 7 * R)], s_q, s_dq, r_dq)
    drain(ks.at[pl.ds(0, 7 * R)], s_k, s_v, s_dk, s_dv, r_dk, r_dv)
    drain(G.at[pl.ds(0, 7)], s_ag)
    drain(rx, s_x)
    drain(rz, s_z)
    drain(rx2, s_x2)
    drain(rz2, s_z2)


def write_out(a, b, c, d, ao, bo, co, do, sem):
    copies = [
        pltpu.make_async_copy(src, dst, sem.at[i])
        for i, (src, dst) in enumerate(((a, ao), (b, bo), (c, co), (d, do)))
    ]
    for copy in copies:
        copy.start()
    for copy in copies:
        copy.wait()


def body(grad_out, queries, keys, values, out_weight, doc_starts):
    vm = pltpu.VMEM
    dma = pltpu.SemaphoreType.DMA
    hbm = pl.BlockSpec(memory_space=pl.ANY)
    scratch = [
        vm((T, F), BF16),
        vm((T, DH), BF16),
        vm((T, DH), BF16),
        vm((DH, T), BF16),
        vm((DH, T), BF16),
        vm((NC, T, CW), BF16),
        vm((NC, F, CW), BF16),
        vm((H, NB, T, B), BF16),
        vm((F, T), BF16),
        vm((NB, T, B), F32),
        vm((T, F), F32),
        vm((T, F), BF16),
        vm((NC - EARLY, F, CW), F32),
        vm((NC, F, CW), BF16),
        vm((2, 3, XR, 512), BF16),
        vm((4, 3, ZR, 256), BF16),
        vm((2, XR, 512), BF16),
        vm((3, ZR, 256), BF16),
        vm((3, XR, 256), BF16),
        vm((3, ZR, 256), BF16),
        vm((ZR, 256), F32),
        vm((NB, B, F), BF16),
        vm((T, DH), F32),
        vm((T, DH), F32),
        vm((T, DH), BF16),
        vm((T, DH), BF16),
    ]
    scratch += [dma] * 9
    scratch += [dma] + [dma((NC,))] * 6 + [dma] * 2
    scratch += [dma] * 6 + [dma((2,)), dma((4,))]
    scratch += [dma] * 9
    shapes = (((R, D), BF16), ((R, 1024), BF16), ((R, 1024), BF16), ((F, 256), F32))
    local = pl.BlockSpec(memory_space=pltpu.VMEM)
    held = pl.pallas_call(
        kernel,
        name="attention_back",
        out_shape=tuple(vm(shape, dtype) for shape, dtype in shapes),
        in_specs=[hbm] * 5 + [pl.BlockSpec(memory_space=pltpu.SMEM)],
        out_specs=(local,) * 4,
        scratch_shapes=scratch,
        compiler_params=pltpu.CompilerParams(
            collective_id=0, has_side_effects=True, vmem_limit_bytes=60 * 1024 * 1024
        ),
    )(grad_out[0], queries[0], keys[0], values[0], out_weight, doc_starts)
    out = pl.pallas_call(
        write_out,
        name="write_out",
        out_shape=tuple(jax.ShapeDtypeStruct(shape, dtype) for shape, dtype in shapes),
        in_specs=[local] * 4,
        out_specs=(hbm,) * 4,
        scratch_shapes=[dma((4,))],
    )(*[pltpu.with_memory_space_constraint(x, pltpu.VMEM) for x in held])
    return (out[0][None], out[1][None], out[2][None], out[3])


def solution(mesh):
    return jax.shard_map(
        body,
        mesh=mesh,
        in_specs=(
            P("dp", "seq", None),
            P("dp", "seq", None),
            P("dp", "seq", None),
            P("dp", "seq", None),
            P("seq", None),
            P("dp", None),
        ),
        out_specs=(
            P("dp", "seq", None),
            P("dp", "seq", None),
            P("dp", "seq", None),
            P("seq", "dp"),
        ),
        check_vma=False,
    )
```

```python
import math

import jax
import jax.numpy as jnp
from jax import lax
from jax.experimental import pallas as pl
from jax.experimental.pallas import tpu as pltpu
from jax.sharding import PartitionSpec as P

MESH = pl.DeviceIdType.MESH
F32 = jnp.float32
BF16 = jnp.bfloat16
T = 1024
R = 128
XR = 320
ZR = 512 - XR
H = 4
DH = 128
F = H * DH
D = 4096
B = 256
NB = T // B
NC = 8
CW = D // NC
CHUNK_X = (2, 2, 1, 3, 1, 3, 0, 0)
EARLY = 4
CHUNK_OWN = (0, 1, 0, 0, 1, 1, 0, 1)
SCALE = 1.0 / math.sqrt(DH)
NT = (((1,), (1,)), ((), ()))


def dot(a, b):
    return jnp.dot(a, b, preferred_element_type=F32)


def dot_nt(a, b):
    return lax.dot_general(a, b, NT, preferred_element_type=F32)


def mult(x, n):
    return pl.multiple_of(x, n)


def kernel(
    go, q, k, v, w, starts,
    dq_o, dk_o, dv_o, wg_o,
    qs, ks, vs, kT, vT, G, ow, PT, OT, bias, dOacc, dO, Wacc, Wb, rx, rz, s1b, s2b, rx2, rz2, fin,
    dqs, dKa, dVa, dkb, dvb,
    s_q, r_q, s_k, r_k, s_v, r_v, l_q, l_k, l_v,
    s_ag, r_m, r_p, r_o, r_own, r_near, r_opp, l_g, l_w,
    s_x, s_z, s_x2, r_x2, s_z2, r_z2, r_x, r_z,
    s_dq, r_dq, s_dk, r_dk, s_dv, r_dv, l_dq, l_dk, l_dv,
):
    dp = lax.axis_index("dp")
    me = lax.axis_index("seq")
    X, Z = dp // 4, lax.rem(dp, 4)
    Y, C = me // 2, lax.rem(me, 2)
    par = lax.rem(Z, 2)

    def seq_dev(s):
        return (dp, s)

    def grid_dev(x, z):
        return (x * 4 + z, me)

    def remote(src, dst, ss, rs, dev):
        return pltpu.make_async_remote_copy(
            src_ref=src, dst_ref=dst, send_sem=ss, recv_sem=rs, device_id=dev, device_id_type=MESH
        )

    up = seq_dev(lax.rem(Y + 1, 4) * 2 + C)
    down = seq_dev(lax.rem(Y + 3, 4) * 2 + C)
    sib = seq_dev(Y * 2 + 1 - C)

    barrier = pltpu.get_barrier_semaphore()
    for o in range(1, 8):
        pl.semaphore_signal(
            barrier, 1, device_id=seq_dev(lax.rem(me + o, 8)), device_id_type=MESH
        )
    for o in range(1, 4):
        pl.semaphore_signal(
            barrier, 1, device_id=grid_dev(lax.rem(X + o, 4), Z), device_id_type=MESH
        )
        pl.semaphore_signal(
            barrier, 1, device_id=grid_dev(X, lax.rem(Z + o, 4)), device_id_type=MESH
        )
    pl.semaphore_wait(barrier, 13)

    my_rows = pl.ds(mult(me * R, R), R)

    for o in (4, 5, 3, 2, 6, 1, 7):
        g = lax.rem(me + o, 8)
        remote(k.at[:, pl.ds(mult(g * DH, DH), DH)], ks.at[my_rows], s_k, r_k, seq_dev(g)).start()
        remote(v.at[:, pl.ds(mult(g * DH, DH), DH)], vs.at[my_rows], s_v, r_v, seq_dev(g)).start()
        remote(q.at[:, pl.ds(mult(g * F, F), F)], qs.at[my_rows], s_q, r_q, seq_dev(g)).start()
    own_q = pltpu.make_async_copy(q.at[:, pl.ds(mult(me * F, F), F)], qs.at[my_rows], l_q)
    own_k = pltpu.make_async_copy(k.at[:, pl.ds(mult(me * DH, DH), DH)], ks.at[my_rows], l_k)
    own_v = pltpu.make_async_copy(v.at[:, pl.ds(mult(me * DH, DH), DH)], vs.at[my_rows], l_v)
    own_q.start()
    own_k.start()
    own_v.start()

    def chunk_cols(j):
        xb = lax.rem(X + CHUNK_X[j], 4)
        zp = Z // 2 if CHUNK_OWN[j] else 1 - Z // 2
        return pl.ds(mult((xb * 2 + zp) * CW, CW), CW)

    def rows_of(s):
        return pl.ds(mult(s * R, R), R)

    def block_of(b):
        return pl.ds(mult(b * B, B), B)

    def send_own(j):
        src = go.at[:, chunk_cols(j)]
        dst = G.at[j, my_rows]
        remote(src, dst, s_ag, r_p.at[j], up).start()
        remote(src, dst, s_ag, r_m.at[j], down).start()

    y_up, y_down, y_opp = lax.rem(Y + 1, 4), lax.rem(Y + 3, 4), lax.rem(Y + 2, 4)
    from_down, from_up, from_opp = y_down * 2 + C, y_up * 2 + C, y_opp * 2 + C

    def piece(j, s):
        return G.at[j, rows_of(s)]

    def arrived(j, s, sem):
        pltpu.make_async_copy(piece(j, s), piece(j, s), sem).wait()

    def relay(j):
        lo, hi = piece(j, from_down), piece(j, from_up)
        if j % 2 == 0:
            arrived(j, from_down, r_p.at[j])
            remote(lo, lo, s_ag, r_o.at[j], up).start()
            arrived(j, from_up, r_m.at[j])
        else:
            arrived(j, from_up, r_m.at[j])
            remote(hi, hi, s_ag, r_o.at[j], down).start()
            arrived(j, from_down, r_p.at[j])
        remote(lo, lo, s_ag, r_near.at[j], sib).start()
        remote(hi, hi, s_ag, r_near.at[j], sib).start()

    for j in range(NC):
        pltpu.make_async_copy(go.at[:, chunk_cols(j)], G.at[j, my_rows], l_g).start()
        pltpu.make_async_copy(w.at[:, chunk_cols(j)], ow.at[j], l_w).start()
    for j in range(4):
        send_own(j)
    for j in range(NC):
        remote(go.at[:, chunk_cols(j)], G.at[j, my_rows], s_ag, r_own.at[j], sib).start()

    for i in range(NB):
        t = i * B + lax.broadcasted_iota(jnp.int32, (1, B), 1)
        opening = jnp.zeros((1, B), jnp.int32)
        for d in range(8):
            s = starts[0, d]
            opening = jnp.maximum(opening, jnp.where(s <= t, s, 0))
        n = (i + 1) * B
        u = lax.broadcasted_iota(jnp.int32, (n, B), 0)
        bias[i, :n] = jnp.where((u >= opening) & (u <= t), 0.0, -1e30)
    dKa[...] = jnp.zeros_like(dKa)
    dVa[...] = jnp.zeros_like(dVa)

    pltpu.make_async_copy(G.at[0], G.at[0], l_g).wait()
    pltpu.make_async_copy(ow, ow, l_w).wait()

    def project(j, b, first):
        rows = block_of(b)
        part = dot_nt(G[j, rows], ow[j])
        dOacc[rows] = part if first else dOacc[rows] + part

    def projected(b):
        rows = block_of(b)
        dO[rows] = dOacc[rows].astype(BF16)

    for j in range(NC):
        arrived(j, me + 1 - 2 * C, r_own.at[j])
        project(j, Y, j == 0)
    projected(Y)

    own_q.wait()
    own_k.wait()
    own_v.wait()
    pltpu.make_async_copy(ks.at[pl.ds(0, 7 * R)], ks.at[pl.ds(0, 7 * R)], r_k).wait()
    pltpu.make_async_copy(vs.at[pl.ds(0, 7 * R)], vs.at[pl.ds(0, 7 * R)], r_v).wait()
    kT[...] = ks[...].T
    vT[...] = vs[...].T
    pltpu.make_async_copy(qs.at[pl.ds(0, 7 * R)], qs.at[pl.ds(0, 7 * R)], r_q).wait()

    for h in range(H):
        cols = pl.ds(h * DH, DH)
        for i in range(NB):
            n = (i + 1) * B
            st = dot_nt(ks[:n], qs[pl.ds(i * B, B), cols])
            st = st * (SCALE * math.log2(math.e)) + bias[i, :n]
            top = jnp.max(st, axis=0, keepdims=True)
            p = jnp.exp2(st - top)
            p = (p * (1.0 / jnp.sum(p, axis=0, keepdims=True))).astype(BF16)
            PT[h, i, :n] = p
            OT[cols, pl.ds(i * B, B)] = dot(vT[:, :n], p).astype(BF16)
        if h < EARLY:
            relay(h)
        send_own(h + 4)

    hc = [pl.ds(h * DH, DH) for h in range(H)]

    my_f = pl.ds(mult(me * F, F), F)
    my_d = pl.ds(mult(me * DH, DH), DH)

    def backward(b, far=True):
        rows = block_of(b)

        def pair(n, g):
            cols = [pl.ds(mult((2 * g + e) * DH, DH), DH) for e in range(2)]
            ps, gs, dss = [], [], []
            for e in range(2):
                grad = dO[rows, cols[e]]
                gT = grad.astype(F32).T
                delta = jnp.sum(gT * OT[cols[e], rows].astype(F32), axis=0, keepdims=True)
                p = PT[2 * g + e, b, :n]
                ds = (p.astype(F32) * (dot_nt(vs[:n], grad) - delta)).astype(BF16)
                dqs[b, :, cols[e]] = (dot(kT[:, :n], ds).T * SCALE).astype(BF16)
                ps.append(p)
                gs.append(grad)
                dss.append(ds)
            dVa[:n] += dot(jnp.concatenate(ps, axis=1), jnp.concatenate(gs, axis=0))
            for c in range(2 if far else 0):
                remote(
                    dqs.at[b, pl.ds(c * R, R), pl.ds(mult(g * B, B), B)],
                    dq_o.at[:, pl.ds(mult(me * F + g * B, B), B)],
                    s_dq, r_dq, seq_dev(b * 2 + c),
                ).start()
            qq = jnp.concatenate([qs[rows, c] for c in cols], axis=0)
            dKa[:n] += dot(jnp.concatenate(dss, axis=1), qq)

        for i in range(NB):

            @pl.when(b == i)
            def _():
                @pl.loop(0, H // 2)
                def _(g):
                    pair((i + 1) * B, g)

    backward(Y, False)
    other_rows = pl.ds(mult((1 - C) * R, R), R)
    own_rows = pl.ds(mult(C * R, R), R)
    remote(dqs.at[Y, other_rows], dq_o.at[:, my_f], s_dq, r_dq, sib).start()
    own_dq = pltpu.make_async_copy(dqs.at[Y, own_rows], dq_o.at[:, my_f], l_dq)
    own_dq.start()

    def opposite(j):
        arrived(j, from_opp, r_o.at[j])
        opp = piece(j, from_opp)
        remote(opp, opp, s_ag, r_opp.at[j], sib).start()

    def near_here(j):
        half = G.at[j, pl.ds(0, 2 * R)]
        pltpu.make_async_copy(half, half, r_near.at[j]).wait()

    other = 1 - Z // 2

    def z_slot(zz):
        return lax.rem(zz - Z + 4, 4) - 1

    def scatter(j):
        dx = CHUNK_X[j]
        if dx:
            remote(
                Wb.at[j, pl.ds(0, XR)], rx.at[CHUNK_OWN[j], dx - 1], s_x, r_x.at[CHUNK_OWN[j]],
                grid_dev(lax.rem(X + dx, 4), Z),
            ).start()
        if CHUNK_OWN[j]:
            sends = [(mult((1 - par) * 256, 256), Z + 1 - 2 * par)]
        else:
            sends = [(c * 256, 2 * other + c) for c in range(2)]
        for col, zz in sends:
            remote(
                Wb.at[j, pl.ds(XR, ZR), pl.ds(col, 256)], rz.at[dx, z_slot(zz)], s_z, r_z.at[dx],
                grid_dev(X, zz),
            ).start()

    def near(j):
        near_here(j)
        s = None
        for b in (Y, y_up, y_down):
            d = dot(OT[:, block_of(b)], G[j, block_of(b)])
            s = d if s is None else s + d
        Wacc[j - EARLY] = s
        for b in (y_up, y_down):
            project(j, b, False)

    def full(j):
        arrived(j, y_opp * 2 + 1 - C, r_opp.at[j])
        near_here(j)
        for b in (y_up, y_down, y_opp):
            project(j, b, j == 0)
        Wb[j] = dot(OT[...], G[j]).astype(BF16)
        scatter(j)

    def finish(j):
        arrived(j, y_opp * 2 + 1 - C, r_opp.at[j])
        project(j, y_opp, False)
        Wb[j] = (Wacc[j - EARLY] + dot(OT[:, block_of(y_opp)], G[j, block_of(y_opp)])).astype(BF16)
        scatter(j)

    opposite(0)
    full(0)
    relay(4)
    opposite(1)
    near(4)
    full(1)
    relay(5)
    near(5)
    opposite(2)
    full(2)
    relay(6)
    opposite(3)
    near(6)
    full(3)
    relay(7)
    near(7)
    projected(y_up)
    projected(y_down)
    backward(y_up)
    opposite(4)
    opposite(5)
    finish(4)
    finish(5)
    backward(y_down)
    opposite(6)
    opposite(7)
    finish(6)
    finish(7)
    projected(y_opp)

    def send_kv(kb):
        rows = pl.ds(kb * B, B)
        dkb[rows] = (dKa[rows] * SCALE).astype(BF16)
        dvb[rows] = dVa[rows].astype(BF16)
        for c in range(2):
            g = kb * 2 + c

            @pl.when(me != g)
            def _():
                remote(dkb.at[rows_of(g)], dk_o.at[:, my_d], s_dk, r_dk, seq_dev(g)).start()
                remote(dvb.at[rows_of(g)], dv_o.at[:, my_d], s_dv, r_dv, seq_dev(g)).start()

    for kb in range(1, NB):

        @pl.when((kb > y_opp) & (kb != Y))
        def _():
            send_kv(kb)

    backward(y_opp)
    for kb in range(NB):

        @pl.when((kb <= y_opp) | (kb == Y))
        def _():
            send_kv(kb)

    own_dk = pltpu.make_async_copy(dkb.at[my_rows], dk_o.at[:, my_d], l_dk)
    own_dv = pltpu.make_async_copy(dvb.at[my_rows], dv_o.at[:, my_d], l_dv)
    own_dk.start()
    own_dv.start()

    chunk_at = {(CHUNK_X[j], CHUNK_OWN[j]): j for j in range(NC)}
    own_cols = pl.ds(mult(par * 256, 256), 256)

    def z_sum(dx):
        pltpu.make_async_copy(rz.at[dx], rz.at[dx], r_z.at[dx]).wait()
        s = Wb[chunk_at[dx, 1], XR:, own_cols].astype(F32)
        for i in range(3):
            s += rz[dx, i].astype(F32)
        if dx:
            s2b[dx - 1] = s.astype(BF16)
            remote(
                s2b.at[dx - 1], rz2.at[dx - 1], s_z2, r_z2, grid_dev(lax.rem(X + dx, 4), Z)
            ).start()
        else:
            fin[...] = s

    def x_sum(e):
        pltpu.make_async_copy(rx.at[e], rx.at[e], r_x.at[e]).wait()
        s = Wb[chunk_at[0, e], :XR].astype(F32)
        for i in range(3):
            s += rx[e, i].astype(F32)
        s1b[e] = s.astype(BF16)
        if e:
            sends = [(mult((1 - par) * 256, 256), Z + 1 - 2 * par)]
        else:
            sends = [(c * 256, 2 * other + c) for c in range(2)]
        for col, zz in sends:
            remote(
                s1b.at[e, :, pl.ds(col, 256)], rx2.at[z_slot(zz)], s_x2, r_x2, grid_dev(X, zz)
            ).start()

    z_sum(2)
    x_sum(0)
    z_sum(1)
    z_sum(3)
    x_sum(1)
    z_sum(0)
    pltpu.make_async_copy(rx2, rx2, r_x2).wait()
    norm = 1.0 / math.sqrt(T * 16)
    s = s1b[1, :, own_cols].astype(F32)
    for i in range(3):
        s += rx2[i].astype(F32)
    wg_o[:XR] = s * norm
    pltpu.make_async_copy(rz2, rz2, r_z2).wait()
    s = fin[...]
    for i in range(3):
        s += rz2[i].astype(F32)
    wg_o[XR:] = s * norm

    def drain(ref, *sems):
        for sem in sems:
            pltpu.make_async_copy(ref, ref, sem).wait()

    own_dq.wait()
    own_dk.wait()
    own_dv.wait()
    drain(qs.at[pl.ds(0, 7 * R)], s_q, s_dq, r_dq)
    drain(ks.at[pl.ds(0, 7 * R)], s_k, s_v, s_dk, s_dv, r_dk, r_dv)
    drain(G.at[pl.ds(0, 7)], s_ag)
    drain(rx, s_x)
    drain(rz, s_z)
    drain(rx2, s_x2)
    drain(rz2, s_z2)


def write_out(a, b, c, d, ao, bo, co, do, sem):
    copies = [
        pltpu.make_async_copy(src, dst, sem.at[i])
        for i, (src, dst) in enumerate(((a, ao), (b, bo), (c, co), (d, do)))
    ]
    for copy in copies:
        copy.start()
    for copy in copies:
        copy.wait()


def body(grad_out, queries, keys, values, out_weight, doc_starts):
    vm = pltpu.VMEM
    dma = pltpu.SemaphoreType.DMA
    hbm = pl.BlockSpec(memory_space=pl.ANY)
    scratch = [
        vm((T, F), BF16),
        vm((T, DH), BF16),
        vm((T, DH), BF16),
        vm((DH, T), BF16),
        vm((DH, T), BF16),
        vm((NC, T, CW), BF16),
        vm((NC, F, CW), BF16),
        vm((H, NB, T, B), BF16),
        vm((F, T), BF16),
        vm((NB, T, B), F32),
        vm((T, F), F32),
        vm((T, F), BF16),
        vm((NC - EARLY, F, CW), F32),
        vm((NC, F, CW), BF16),
        vm((2, 3, XR, 512), BF16),
        vm((4, 3, ZR, 256), BF16),
        vm((2, XR, 512), BF16),
        vm((3, ZR, 256), BF16),
        vm((3, XR, 256), BF16),
        vm((3, ZR, 256), BF16),
        vm((ZR, 256), F32),
        vm((NB, B, F), BF16),
        vm((T, DH), F32),
        vm((T, DH), F32),
        vm((T, DH), BF16),
        vm((T, DH), BF16),
    ]
    scratch += [dma] * 9
    scratch += [dma] + [dma((NC,))] * 6 + [dma] * 2
    scratch += [dma] * 6 + [dma((2,)), dma((4,))]
    scratch += [dma] * 9
    shapes = (((R, D), BF16), ((R, 1024), BF16), ((R, 1024), BF16), ((F, 256), F32))
    local = pl.BlockSpec(memory_space=pltpu.VMEM)
    held = pl.pallas_call(
        kernel,
        name="attention_back",
        out_shape=tuple(vm(shape, dtype) for shape, dtype in shapes),
        in_specs=[hbm] * 5 + [pl.BlockSpec(memory_space=pltpu.SMEM)],
        out_specs=(local,) * 4,
        scratch_shapes=scratch,
        compiler_params=pltpu.CompilerParams(
            collective_id=0, has_side_effects=True, vmem_limit_bytes=60 * 1024 * 1024
        ),
    )(grad_out[0], queries[0], keys[0], values[0], out_weight, doc_starts)
    out = pl.pallas_call(
        write_out,
        name="write_out",
        out_shape=tuple(jax.ShapeDtypeStruct(shape, dtype) for shape, dtype in shapes),
        in_specs=[local] * 4,
        out_specs=(hbm,) * 4,
        scratch_shapes=[dma((4,))],
    )(*[pltpu.with_memory_space_constraint(x, pltpu.VMEM) for x in held])
    return (out[0][None], out[1][None], out[2][None], out[3])


def solution(mesh):
    return jax.shard_map(
        body,
        mesh=mesh,
        in_specs=(
            P("dp", "seq", None),
            P("dp", "seq", None),
            P("dp", "seq", None),
            P("dp", "seq", None),
            P("seq", None),
            P("dp", None),
        ),
        out_specs=(
            P("dp", "seq", None),
            P("dp", "seq", None),
            P("dp", "seq", None),
            P("seq", "dp"),
        ),
        check_vma=False,
    )
```

```python
import math

import jax
import jax.numpy as jnp
from jax import lax
from jax.experimental import pallas as pl
from jax.experimental.pallas import tpu as pltpu
from jax.sharding import PartitionSpec as P

MESH = pl.DeviceIdType.MESH
F32 = jnp.float32
BF16 = jnp.bfloat16
T = 1024
R = 128
XR = 320
ZR = 512 - XR
H = 4
DH = 128
F = H * DH
D = 4096
B = 256
NB = T // B
NC = 8
CW = D // NC
CHUNK_X = (2, 2, 1, 3, 1, 3, 0, 0)
EARLY = 2
CHUNK_OWN = (0, 1, 0, 0, 1, 1, 0, 1)
SCALE = 1.0 / math.sqrt(DH)
NT = (((1,), (1,)), ((), ()))


def dot(a, b):
    return jnp.dot(a, b, preferred_element_type=F32)


def dot_nt(a, b):
    return lax.dot_general(a, b, NT, preferred_element_type=F32)


def mult(x, n):
    return pl.multiple_of(x, n)


def kernel(
    go, q, k, v, w, starts,
    dq_o, dk_o, dv_o, wg_o,
    qs, ks, vs, kT, vT, G, ow, PT, OT, bias, dOacc, dO, Wacc, Wb, rx, rz, s1b, s2b, rx2, rz2, fin,
    dqs, dKa, dVa, dkb, dvb,
    s_q, r_q, s_k, r_k, s_v, r_v, l_q, l_k, l_v,
    s_ag, r_m, r_p, r_o, r_own, r_near, r_opp, l_g, l_w,
    s_x, s_z, s_x2, r_x2, s_z2, r_z2, r_x, r_z,
    s_dq, r_dq, s_dk, r_dk, s_dv, r_dv, l_dq, l_dk, l_dv,
):
    dp = lax.axis_index("dp")
    me = lax.axis_index("seq")
    X, Z = dp // 4, lax.rem(dp, 4)
    Y, C = me // 2, lax.rem(me, 2)
    par = lax.rem(Z, 2)

    def seq_dev(s):
        return (dp, s)

    def grid_dev(x, z):
        return (x * 4 + z, me)

    def remote(src, dst, ss, rs, dev):
        return pltpu.make_async_remote_copy(
            src_ref=src, dst_ref=dst, send_sem=ss, recv_sem=rs, device_id=dev, device_id_type=MESH
        )

    up = seq_dev(lax.rem(Y + 1, 4) * 2 + C)
    down = seq_dev(lax.rem(Y + 3, 4) * 2 + C)
    sib = seq_dev(Y * 2 + 1 - C)

    barrier = pltpu.get_barrier_semaphore()
    for o in range(1, 8):
        pl.semaphore_signal(
            barrier, 1, device_id=seq_dev(lax.rem(me + o, 8)), device_id_type=MESH
        )
    for o in range(1, 4):
        pl.semaphore_signal(
            barrier, 1, device_id=grid_dev(lax.rem(X + o, 4), Z), device_id_type=MESH
        )
        pl.semaphore_signal(
            barrier, 1, device_id=grid_dev(X, lax.rem(Z + o, 4)), device_id_type=MESH
        )
    pl.semaphore_wait(barrier, 13)

    my_rows = pl.ds(mult(me * R, R), R)

    for o in (4, 5, 3, 2, 6, 1, 7):
        g = lax.rem(me + o, 8)
        remote(k.at[:, pl.ds(mult(g * DH, DH), DH)], ks.at[my_rows], s_k, r_k, seq_dev(g)).start()
        remote(v.at[:, pl.ds(mult(g * DH, DH), DH)], vs.at[my_rows], s_v, r_v, seq_dev(g)).start()
        remote(q.at[:, pl.ds(mult(g * F, F), F)], qs.at[my_rows], s_q, r_q, seq_dev(g)).start()
    own_q = pltpu.make_async_copy(q.at[:, pl.ds(mult(me * F, F), F)], qs.at[my_rows], l_q)
    own_k = pltpu.make_async_copy(k.at[:, pl.ds(mult(me * DH, DH), DH)], ks.at[my_rows], l_k)
    own_v = pltpu.make_async_copy(v.at[:, pl.ds(mult(me * DH, DH), DH)], vs.at[my_rows], l_v)
    own_q.start()
    own_k.start()
    own_v.start()

    def chunk_cols(j):
        xb = lax.rem(X + CHUNK_X[j], 4)
        zp = Z // 2 if CHUNK_OWN[j] else 1 - Z // 2
        return pl.ds(mult((xb * 2 + zp) * CW, CW), CW)

    def rows_of(s):
        return pl.ds(mult(s * R, R), R)

    def block_of(b):
        return pl.ds(mult(b * B, B), B)

    def send_own(j):
        src = go.at[:, chunk_cols(j)]
        dst = G.at[j, my_rows]
        remote(src, dst, s_ag, r_p.at[j], up).start()
        remote(src, dst, s_ag, r_m.at[j], down).start()

    y_up, y_down, y_opp = lax.rem(Y + 1, 4), lax.rem(Y + 3, 4), lax.rem(Y + 2, 4)
    from_down, from_up, from_opp = y_down * 2 + C, y_up * 2 + C, y_opp * 2 + C

    def piece(j, s):
        return G.at[j, rows_of(s)]

    def arrived(j, s, sem):
        pltpu.make_async_copy(piece(j, s), piece(j, s), sem).wait()

    def relay(j):
        lo, hi = piece(j, from_down), piece(j, from_up)
        if j % 2 == 0:
            arrived(j, from_down, r_p.at[j])
            remote(lo, lo, s_ag, r_o.at[j], up).start()
            arrived(j, from_up, r_m.at[j])
        else:
            arrived(j, from_up, r_m.at[j])
            remote(hi, hi, s_ag, r_o.at[j], down).start()
            arrived(j, from_down, r_p.at[j])
        remote(lo, lo, s_ag, r_near.at[j], sib).start()
        remote(hi, hi, s_ag, r_near.at[j], sib).start()

    for j in range(NC):
        pltpu.make_async_copy(go.at[:, chunk_cols(j)], G.at[j, my_rows], l_g).start()
        pltpu.make_async_copy(w.at[:, chunk_cols(j)], ow.at[j], l_w).start()
    for j in range(4):
        send_own(j)
    for j in range(NC):
        remote(go.at[:, chunk_cols(j)], G.at[j, my_rows], s_ag, r_own.at[j], sib).start()

    for i in range(NB):
        t = i * B + lax.broadcasted_iota(jnp.int32, (1, B), 1)
        opening = jnp.zeros((1, B), jnp.int32)
        for d in range(8):
            s = starts[0, d]
            opening = jnp.maximum(opening, jnp.where(s <= t, s, 0))
        n = (i + 1) * B
        u = lax.broadcasted_iota(jnp.int32, (n, B), 0)
        bias[i, :n] = jnp.where((u >= opening) & (u <= t), 0.0, -1e30)
    dKa[...] = jnp.zeros_like(dKa)
    dVa[...] = jnp.zeros_like(dVa)

    pltpu.make_async_copy(G.at[0], G.at[0], l_g).wait()
    pltpu.make_async_copy(ow, ow, l_w).wait()

    def project(j, b, first):
        rows = block_of(b)
        part = dot_nt(G[j, rows], ow[j])
        dOacc[rows] = part if first else dOacc[rows] + part

    def projected(b):
        rows = block_of(b)
        dO[rows] = dOacc[rows].astype(BF16)

    for j in range(NC):
        arrived(j, me + 1 - 2 * C, r_own.at[j])
        project(j, Y, j == 0)
    projected(Y)

    own_q.wait()
    own_k.wait()
    own_v.wait()
    pltpu.make_async_copy(ks.at[pl.ds(0, 7 * R)], ks.at[pl.ds(0, 7 * R)], r_k).wait()
    pltpu.make_async_copy(vs.at[pl.ds(0, 7 * R)], vs.at[pl.ds(0, 7 * R)], r_v).wait()
    kT[...] = ks[...].T
    vT[...] = vs[...].T
    pltpu.make_async_copy(qs.at[pl.ds(0, 7 * R)], qs.at[pl.ds(0, 7 * R)], r_q).wait()

    for h in range(H):
        cols = pl.ds(h * DH, DH)
        for i in range(NB):
            n = (i + 1) * B
            st = dot_nt(ks[:n], qs[pl.ds(i * B, B), cols])
            st = st * (SCALE * math.log2(math.e)) + bias[i, :n]
            top = jnp.max(st, axis=0, keepdims=True)
            p = jnp.exp2(st - top)
            p = (p * (1.0 / jnp.sum(p, axis=0, keepdims=True))).astype(BF16)
            PT[h, i, :n] = p
            OT[cols, pl.ds(i * B, B)] = dot(vT[:, :n], p).astype(BF16)
        if h < EARLY:
            relay(h)
        send_own(h + 4)

    hc = [pl.ds(h * DH, DH) for h in range(H)]

    my_f = pl.ds(mult(me * F, F), F)
    my_d = pl.ds(mult(me * DH, DH), DH)

    def backward(b, far=True):
        rows = block_of(b)

        def pair(n, g):
            cols = [pl.ds(mult((2 * g + e) * DH, DH), DH) for e in range(2)]
            ps, gs, dss = [], [], []
            for e in range(2):
                grad = dO[rows, cols[e]]
                gT = grad.astype(F32).T
                delta = jnp.sum(gT * OT[cols[e], rows].astype(F32), axis=0, keepdims=True)
                p = PT[2 * g + e, b, :n]
                ds = (p.astype(F32) * (dot_nt(vs[:n], grad) - delta)).astype(BF16)
                dqs[b, :, cols[e]] = (dot(kT[:, :n], ds).T * SCALE).astype(BF16)
                ps.append(p)
                gs.append(grad)
                dss.append(ds)
            dVa[:n] += dot(jnp.concatenate(ps, axis=1), jnp.concatenate(gs, axis=0))
            for c in range(2 if far else 0):
                remote(
                    dqs.at[b, pl.ds(c * R, R), pl.ds(mult(g * B, B), B)],
                    dq_o.at[:, pl.ds(mult(me * F + g * B, B), B)],
                    s_dq, r_dq, seq_dev(b * 2 + c),
                ).start()
            qq = jnp.concatenate([qs[rows, c] for c in cols], axis=0)
            dKa[:n] += dot(jnp.concatenate(dss, axis=1), qq)

        for i in range(NB):

            @pl.when(b == i)
            def _():
                @pl.loop(0, H // 2)
                def _(g):
                    pair((i + 1) * B, g)

    backward(Y, False)
    other_rows = pl.ds(mult((1 - C) * R, R), R)
    own_rows = pl.ds(mult(C * R, R), R)
    remote(dqs.at[Y, other_rows], dq_o.at[:, my_f], s_dq, r_dq, sib).start()
    own_dq = pltpu.make_async_copy(dqs.at[Y, own_rows], dq_o.at[:, my_f], l_dq)
    own_dq.start()

    def opposite(j):
        arrived(j, from_opp, r_o.at[j])
        opp = piece(j, from_opp)
        remote(opp, opp, s_ag, r_opp.at[j], sib).start()

    def near_here(j):
        half = G.at[j, pl.ds(0, 2 * R)]
        pltpu.make_async_copy(half, half, r_near.at[j]).wait()

    other = 1 - Z // 2

    def z_slot(zz):
        return lax.rem(zz - Z + 4, 4) - 1

    def scatter(j):
        dx = CHUNK_X[j]
        if dx:
            remote(
                Wb.at[j, pl.ds(0, XR)], rx.at[CHUNK_OWN[j], dx - 1], s_x, r_x.at[CHUNK_OWN[j]],
                grid_dev(lax.rem(X + dx, 4), Z),
            ).start()
        if CHUNK_OWN[j]:
            sends = [(mult((1 - par) * 256, 256), Z + 1 - 2 * par)]
        else:
            sends = [(c * 256, 2 * other + c) for c in range(2)]
        for col, zz in sends:
            remote(
                Wb.at[j, pl.ds(XR, ZR), pl.ds(col, 256)], rz.at[dx, z_slot(zz)], s_z, r_z.at[dx],
                grid_dev(X, zz),
            ).start()

    def near(j):
        near_here(j)
        s = None
        for b in (Y, y_up, y_down):
            d = dot(OT[:, block_of(b)], G[j, block_of(b)])
            s = d if s is None else s + d
        Wacc[j - EARLY] = s
        for b in (y_up, y_down):
            project(j, b, False)

    def full(j):
        arrived(j, y_opp * 2 + 1 - C, r_opp.at[j])
        near_here(j)
        for b in (y_up, y_down, y_opp):
            project(j, b, j == 0)
        Wb[j] = dot(OT[...], G[j]).astype(BF16)
        scatter(j)

    def finish(j):
        arrived(j, y_opp * 2 + 1 - C, r_opp.at[j])
        project(j, y_opp, False)
        Wb[j] = (Wacc[j - EARLY] + dot(OT[:, block_of(y_opp)], G[j, block_of(y_opp)])).astype(BF16)
        scatter(j)

    relay(2)
    relay(3)
    opposite(0)
    full(0)
    opposite(1)
    relay(4)
    near(2)
    full(1)
    relay(5)
    near(3)
    near(4)
    relay(6)
    near(5)
    relay(7)
    near(6)
    near(7)
    projected(y_up)
    projected(y_down)
    opposite(2)
    opposite(3)
    backward(y_up)
    finish(2)
    finish(3)
    opposite(4)
    opposite(5)
    backward(y_down)
    opposite(6)
    opposite(7)
    for j in range(4, NC):
        finish(j)
    projected(y_opp)
    def send_kv(kb):
        rows = pl.ds(kb * B, B)
        dkb[rows] = (dKa[rows] * SCALE).astype(BF16)
        dvb[rows] = dVa[rows].astype(BF16)
        for c in range(2):
            g = kb * 2 + c

            @pl.when(me != g)
            def _():
                remote(dkb.at[rows_of(g)], dk_o.at[:, my_d], s_dk, r_dk, seq_dev(g)).start()
                remote(dvb.at[rows_of(g)], dv_o.at[:, my_d], s_dv, r_dv, seq_dev(g)).start()

    for kb in range(1, NB):

        @pl.when((kb > y_opp) & (kb != Y))
        def _():
            send_kv(kb)

    backward(y_opp)
    for kb in range(NB):

        @pl.when((kb <= y_opp) | (kb == Y))
        def _():
            send_kv(kb)

    own_dk = pltpu.make_async_copy(dkb.at[my_rows], dk_o.at[:, my_d], l_dk)
    own_dv = pltpu.make_async_copy(dvb.at[my_rows], dv_o.at[:, my_d], l_dv)
    own_dk.start()
    own_dv.start()

    chunk_at = {(CHUNK_X[j], CHUNK_OWN[j]): j for j in range(NC)}
    own_cols = pl.ds(mult(par * 256, 256), 256)

    def z_sum(dx):
        pltpu.make_async_copy(rz.at[dx], rz.at[dx], r_z.at[dx]).wait()
        s = Wb[chunk_at[dx, 1], XR:, own_cols].astype(F32)
        for i in range(3):
            s += rz[dx, i].astype(F32)
        if dx:
            s2b[dx - 1] = s.astype(BF16)
            remote(
                s2b.at[dx - 1], rz2.at[dx - 1], s_z2, r_z2, grid_dev(lax.rem(X + dx, 4), Z)
            ).start()
        else:
            fin[...] = s

    def x_sum(e):
        pltpu.make_async_copy(rx.at[e], rx.at[e], r_x.at[e]).wait()
        s = Wb[chunk_at[0, e], :XR].astype(F32)
        for i in range(3):
            s += rx[e, i].astype(F32)
        s1b[e] = s.astype(BF16)
        if e:
            sends = [(mult((1 - par) * 256, 256), Z + 1 - 2 * par)]
        else:
            sends = [(c * 256, 2 * other + c) for c in range(2)]
        for col, zz in sends:
            remote(
                s1b.at[e, :, pl.ds(col, 256)], rx2.at[z_slot(zz)], s_x2, r_x2, grid_dev(X, zz)
            ).start()

    z_sum(2)
    x_sum(0)
    z_sum(1)
    z_sum(3)
    x_sum(1)
    z_sum(0)
    pltpu.make_async_copy(rx2, rx2, r_x2).wait()
    norm = 1.0 / math.sqrt(T * 16)
    s = s1b[1, :, own_cols].astype(F32)
    for i in range(3):
        s += rx2[i].astype(F32)
    wg_o[:XR] = s * norm
    pltpu.make_async_copy(rz2, rz2, r_z2).wait()
    s = fin[...]
    for i in range(3):
        s += rz2[i].astype(F32)
    wg_o[XR:] = s * norm

    def drain(ref, *sems):
        for sem in sems:
            pltpu.make_async_copy(ref, ref, sem).wait()

    own_dq.wait()
    own_dk.wait()
    own_dv.wait()
    drain(qs.at[pl.ds(0, 7 * R)], s_q, s_dq, r_dq)
    drain(ks.at[pl.ds(0, 7 * R)], s_k, s_v, s_dk, s_dv, r_dk, r_dv)
    drain(G.at[pl.ds(0, 7)], s_ag)
    drain(rx, s_x)
    drain(rz, s_z)
    drain(rx2, s_x2)
    drain(rz2, s_z2)


def write_out(a, b, c, d, ao, bo, co, do, sem):
    copies = [
        pltpu.make_async_copy(src, dst, sem.at[i])
        for i, (src, dst) in enumerate(((a, ao), (b, bo), (c, co), (d, do)))
    ]
    for copy in copies:
        copy.start()
    for copy in copies:
        copy.wait()


def body(grad_out, queries, keys, values, out_weight, doc_starts):
    vm = pltpu.VMEM
    dma = pltpu.SemaphoreType.DMA
    hbm = pl.BlockSpec(memory_space=pl.ANY)
    scratch = [
        vm((T, F), BF16),
        vm((T, DH), BF16),
        vm((T, DH), BF16),
        vm((DH, T), BF16),
        vm((DH, T), BF16),
        vm((NC, T, CW), BF16),
        vm((NC, F, CW), BF16),
        vm((H, NB, T, B), BF16),
        vm((F, T), BF16),
        vm((NB, T, B), F32),
        vm((T, F), F32),
        vm((T, F), BF16),
        vm((NC - EARLY, F, CW), F32),
        vm((NC, F, CW), BF16),
        vm((2, 3, XR, 512), BF16),
        vm((4, 3, ZR, 256), BF16),
        vm((2, XR, 512), BF16),
        vm((3, ZR, 256), BF16),
        vm((3, XR, 256), BF16),
        vm((3, ZR, 256), BF16),
        vm((ZR, 256), F32),
        vm((NB, B, F), BF16),
        vm((T, DH), F32),
        vm((T, DH), F32),
        vm((T, DH), BF16),
        vm((T, DH), BF16),
    ]
    scratch += [dma] * 9
    scratch += [dma] + [dma((NC,))] * 6 + [dma] * 2
    scratch += [dma] * 6 + [dma((2,)), dma((4,))]
    scratch += [dma] * 9
    shapes = (((R, D), BF16), ((R, 1024), BF16), ((R, 1024), BF16), ((F, 256), F32))
    local = pl.BlockSpec(memory_space=pltpu.VMEM)
    held = pl.pallas_call(
        kernel,
        name="attention_back",
        out_shape=tuple(vm(shape, dtype) for shape, dtype in shapes),
        in_specs=[hbm] * 5 + [pl.BlockSpec(memory_space=pltpu.SMEM)],
        out_specs=(local,) * 4,
        scratch_shapes=scratch,
        compiler_params=pltpu.CompilerParams(
            collective_id=0, has_side_effects=True, vmem_limit_bytes=60 * 1024 * 1024
        ),
    )(grad_out[0], queries[0], keys[0], values[0], out_weight, doc_starts)
    out = pl.pallas_call(
        write_out,
        name="write_out",
        out_shape=tuple(jax.ShapeDtypeStruct(shape, dtype) for shape, dtype in shapes),
        in_specs=[local] * 4,
        out_specs=(hbm,) * 4,
        scratch_shapes=[dma((4,))],
    )(*[pltpu.with_memory_space_constraint(x, pltpu.VMEM) for x in held])
    return (out[0][None], out[1][None], out[2][None], out[3])


def solution(mesh):
    return jax.shard_map(
        body,
        mesh=mesh,
        in_specs=(
            P("dp", "seq", None),
            P("dp", "seq", None),
            P("dp", "seq", None),
            P("dp", "seq", None),
            P("seq", None),
            P("dp", None),
        ),
        out_specs=(
            P("dp", "seq", None),
            P("dp", "seq", None),
            P("dp", "seq", None),
            P("seq", "dp"),
        ),
        check_vma=False,
    )
```

```python
import math

import jax
import jax.numpy as jnp
from jax import lax
from jax.experimental import pallas as pl
from jax.experimental.pallas import tpu as pltpu
from jax.sharding import PartitionSpec as P

MESH = pl.DeviceIdType.MESH
F32 = jnp.float32
BF16 = jnp.bfloat16
T = 1024
R = 128
XR = 352
ZR = 512 - XR
H = 4
DH = 128
F = H * DH
D = 4096
B = 256
NB = T // B
NC = 8
CW = D // NC
CHUNK_X = (2, 2, 1, 3, 1, 3, 0, 0)
EARLY = 2
CHUNK_OWN = (0, 1, 0, 0, 1, 1, 0, 1)
SCALE = 1.0 / math.sqrt(DH)
NT = (((1,), (1,)), ((), ()))


def dot(a, b):
    return jnp.dot(a, b, preferred_element_type=F32)


def dot_nt(a, b):
    return lax.dot_general(a, b, NT, preferred_element_type=F32)


def mult(x, n):
    return pl.multiple_of(x, n)


def kernel(
    go, q, k, v, w, starts,
    dq_o, dk_o, dv_o, wg_o,
    qs, ks, vs, kT, vT, G, ow, PT, OT, bias, dOacc, dO, Wacc, Wb, rx, rz, s1b, s2b, rx2, rz2, fin,
    dqs, dKa, dVa, dkb, dvb,
    s_q, r_q, s_k, r_k, s_v, r_v, l_q, l_k, l_v,
    s_ag, r_m, r_p, r_o, r_own, r_near, r_opp, l_g, l_w,
    s_x, s_z, s_x2, r_x2, s_z2, r_z2, r_x, r_z,
    s_dq, r_dq, s_dk, r_dk, s_dv, r_dv, l_dq, l_dk, l_dv,
):
    dp = lax.axis_index("dp")
    me = lax.axis_index("seq")
    X, Z = dp // 4, lax.rem(dp, 4)
    Y, C = me // 2, lax.rem(me, 2)
    par = lax.rem(Z, 2)

    def seq_dev(s):
        return (dp, s)

    def grid_dev(x, z):
        return (x * 4 + z, me)

    def remote(src, dst, ss, rs, dev):
        return pltpu.make_async_remote_copy(
            src_ref=src, dst_ref=dst, send_sem=ss, recv_sem=rs, device_id=dev, device_id_type=MESH
        )

    up = seq_dev(lax.rem(Y + 1, 4) * 2 + C)
    down = seq_dev(lax.rem(Y + 3, 4) * 2 + C)
    sib = seq_dev(Y * 2 + 1 - C)

    barrier = pltpu.get_barrier_semaphore()
    for o in range(1, 8):
        pl.semaphore_signal(
            barrier, 1, device_id=seq_dev(lax.rem(me + o, 8)), device_id_type=MESH
        )
    for o in range(1, 4):
        pl.semaphore_signal(
            barrier, 1, device_id=grid_dev(lax.rem(X + o, 4), Z), device_id_type=MESH
        )
        pl.semaphore_signal(
            barrier, 1, device_id=grid_dev(X, lax.rem(Z + o, 4)), device_id_type=MESH
        )
    pl.semaphore_wait(barrier, 13)

    my_rows = pl.ds(mult(me * R, R), R)

    for o in (4, 5, 3, 2, 6, 1, 7):
        g = lax.rem(me + o, 8)
        remote(k.at[:, pl.ds(mult(g * DH, DH), DH)], ks.at[my_rows], s_k, r_k, seq_dev(g)).start()
        remote(v.at[:, pl.ds(mult(g * DH, DH), DH)], vs.at[my_rows], s_v, r_v, seq_dev(g)).start()
        remote(q.at[:, pl.ds(mult(g * F, F), F)], qs.at[my_rows], s_q, r_q, seq_dev(g)).start()
    own_q = pltpu.make_async_copy(q.at[:, pl.ds(mult(me * F, F), F)], qs.at[my_rows], l_q)
    own_k = pltpu.make_async_copy(k.at[:, pl.ds(mult(me * DH, DH), DH)], ks.at[my_rows], l_k)
    own_v = pltpu.make_async_copy(v.at[:, pl.ds(mult(me * DH, DH), DH)], vs.at[my_rows], l_v)
    own_q.start()
    own_k.start()
    own_v.start()

    def chunk_cols(j):
        xb = lax.rem(X + CHUNK_X[j], 4)
        zp = Z // 2 if CHUNK_OWN[j] else 1 - Z // 2
        return pl.ds(mult((xb * 2 + zp) * CW, CW), CW)

    def rows_of(s):
        return pl.ds(mult(s * R, R), R)

    def block_of(b):
        return pl.ds(mult(b * B, B), B)

    def send_own(j):
        src = go.at[:, chunk_cols(j)]
        dst = G.at[j, my_rows]
        remote(src, dst, s_ag, r_p.at[j], up).start()
        remote(src, dst, s_ag, r_m.at[j], down).start()

    y_up, y_down, y_opp = lax.rem(Y + 1, 4), lax.rem(Y + 3, 4), lax.rem(Y + 2, 4)
    from_down, from_up, from_opp = y_down * 2 + C, y_up * 2 + C, y_opp * 2 + C

    def piece(j, s):
        return G.at[j, rows_of(s)]

    def arrived(j, s, sem):
        pltpu.make_async_copy(piece(j, s), piece(j, s), sem).wait()

    def relay(j):
        lo, hi = piece(j, from_down), piece(j, from_up)
        if j % 2 == 0:
            arrived(j, from_down, r_p.at[j])
            remote(lo, lo, s_ag, r_o.at[j], up).start()
            arrived(j, from_up, r_m.at[j])
        else:
            arrived(j, from_up, r_m.at[j])
            remote(hi, hi, s_ag, r_o.at[j], down).start()
            arrived(j, from_down, r_p.at[j])
        remote(lo, lo, s_ag, r_near.at[j], sib).start()
        remote(hi, hi, s_ag, r_near.at[j], sib).start()

    for j in range(NC):
        pltpu.make_async_copy(go.at[:, chunk_cols(j)], G.at[j, my_rows], l_g).start()
        pltpu.make_async_copy(w.at[:, chunk_cols(j)], ow.at[j], l_w).start()
    for j in range(4):
        send_own(j)
    for j in range(NC):
        remote(go.at[:, chunk_cols(j)], G.at[j, my_rows], s_ag, r_own.at[j], sib).start()

    for i in range(NB):
        t = i * B + lax.broadcasted_iota(jnp.int32, (1, B), 1)
        opening = jnp.zeros((1, B), jnp.int32)
        for d in range(8):
            s = starts[0, d]
            opening = jnp.maximum(opening, jnp.where(s <= t, s, 0))
        n = (i + 1) * B
        u = lax.broadcasted_iota(jnp.int32, (n, B), 0)
        bias[i, :n] = jnp.where((u >= opening) & (u <= t), 0.0, -1e30)
    dKa[...] = jnp.zeros_like(dKa)
    dVa[...] = jnp.zeros_like(dVa)

    pltpu.make_async_copy(G.at[0], G.at[0], l_g).wait()
    pltpu.make_async_copy(ow, ow, l_w).wait()

    def project(j, b, first):
        rows = block_of(b)
        part = dot_nt(G[j, rows], ow[j])
        dOacc[rows] = part if first else dOacc[rows] + part

    def projected(b):
        rows = block_of(b)
        dO[rows] = dOacc[rows].astype(BF16)

    for j in range(NC):
        arrived(j, me + 1 - 2 * C, r_own.at[j])
        project(j, Y, j == 0)
    projected(Y)

    own_q.wait()
    own_k.wait()
    own_v.wait()
    pltpu.make_async_copy(ks.at[pl.ds(0, 7 * R)], ks.at[pl.ds(0, 7 * R)], r_k).wait()
    pltpu.make_async_copy(vs.at[pl.ds(0, 7 * R)], vs.at[pl.ds(0, 7 * R)], r_v).wait()
    kT[...] = ks[...].T
    vT[...] = vs[...].T
    pltpu.make_async_copy(qs.at[pl.ds(0, 7 * R)], qs.at[pl.ds(0, 7 * R)], r_q).wait()

    for h in range(H):
        cols = pl.ds(h * DH, DH)
        for i in range(NB):
            n = (i + 1) * B
            st = dot_nt(ks[:n], qs[pl.ds(i * B, B), cols])
            st = st * (SCALE * math.log2(math.e)) + bias[i, :n]
            top = jnp.max(st, axis=0, keepdims=True)
            p = jnp.exp2(st - top)
            p = (p * (1.0 / jnp.sum(p, axis=0, keepdims=True))).astype(BF16)
            PT[h, i, :n] = p
            OT[cols, pl.ds(i * B, B)] = dot(vT[:, :n], p).astype(BF16)
        if h < EARLY:
            relay(h)
        send_own(h + 4)

    hc = [pl.ds(h * DH, DH) for h in range(H)]

    my_f = pl.ds(mult(me * F, F), F)
    my_d = pl.ds(mult(me * DH, DH), DH)

    def backward(b, far=True):
        rows = block_of(b)

        def pair(n, g):
            cols = [pl.ds(mult((2 * g + e) * DH, DH), DH) for e in range(2)]
            ps, gs, dss = [], [], []
            for e in range(2):
                grad = dO[rows, cols[e]]
                gT = grad.astype(F32).T
                delta = jnp.sum(gT * OT[cols[e], rows].astype(F32), axis=0, keepdims=True)
                p = PT[2 * g + e, b, :n]
                ds = (p.astype(F32) * (dot_nt(vs[:n], grad) - delta)).astype(BF16)
                dqs[b, :, cols[e]] = (dot(kT[:, :n], ds).T * SCALE).astype(BF16)
                ps.append(p)
                gs.append(grad)
                dss.append(ds)
            dVa[:n] += dot(jnp.concatenate(ps, axis=1), jnp.concatenate(gs, axis=0))
            for c in range(2 if far else 0):
                remote(
                    dqs.at[b, pl.ds(c * R, R), pl.ds(mult(g * B, B), B)],
                    dq_o.at[:, pl.ds(mult(me * F + g * B, B), B)],
                    s_dq, r_dq, seq_dev(b * 2 + c),
                ).start()
            qq = jnp.concatenate([qs[rows, c] for c in cols], axis=0)
            dKa[:n] += dot(jnp.concatenate(dss, axis=1), qq)

        for i in range(NB):

            @pl.when(b == i)
            def _():
                @pl.loop(0, H // 2)
                def _(g):
                    pair((i + 1) * B, g)

    backward(Y, False)
    other_rows = pl.ds(mult((1 - C) * R, R), R)
    own_rows = pl.ds(mult(C * R, R), R)
    remote(dqs.at[Y, other_rows], dq_o.at[:, my_f], s_dq, r_dq, sib).start()
    own_dq = pltpu.make_async_copy(dqs.at[Y, own_rows], dq_o.at[:, my_f], l_dq)
    own_dq.start()

    def opposite(j):
        arrived(j, from_opp, r_o.at[j])
        opp = piece(j, from_opp)
        remote(opp, opp, s_ag, r_opp.at[j], sib).start()

    def near_here(j):
        half = G.at[j, pl.ds(0, 2 * R)]
        pltpu.make_async_copy(half, half, r_near.at[j]).wait()

    other = 1 - Z // 2

    def z_slot(zz):
        return lax.rem(zz - Z + 4, 4) - 1

    def scatter(j):
        dx = CHUNK_X[j]
        if dx:
            remote(
                Wb.at[j, pl.ds(0, XR)], rx.at[CHUNK_OWN[j], dx - 1], s_x, r_x.at[CHUNK_OWN[j]],
                grid_dev(lax.rem(X + dx, 4), Z),
            ).start()
        if CHUNK_OWN[j]:
            sends = [(mult((1 - par) * 256, 256), Z + 1 - 2 * par)]
        else:
            sends = [(c * 256, 2 * other + c) for c in range(2)]
        for col, zz in sends:
            remote(
                Wb.at[j, pl.ds(XR, ZR), pl.ds(col, 256)], rz.at[dx, z_slot(zz)], s_z, r_z.at[dx],
                grid_dev(X, zz),
            ).start()

    def near(j):
        near_here(j)
        s = None
        for b in (Y, y_up, y_down):
            d = dot(OT[:, block_of(b)], G[j, block_of(b)])
            s = d if s is None else s + d
        Wacc[j - EARLY] = s
        for b in (y_up, y_down):
            project(j, b, False)

    def full(j):
        arrived(j, y_opp * 2 + 1 - C, r_opp.at[j])
        near_here(j)
        for b in (y_up, y_down, y_opp):
            project(j, b, j == 0)
        Wb[j] = dot(OT[...], G[j]).astype(BF16)
        scatter(j)

    def finish(j):
        arrived(j, y_opp * 2 + 1 - C, r_opp.at[j])
        project(j, y_opp, False)
        Wb[j] = (Wacc[j - EARLY] + dot(OT[:, block_of(y_opp)], G[j, block_of(y_opp)])).astype(BF16)
        scatter(j)

    relay(2)
    relay(3)
    opposite(0)
    full(0)
    opposite(1)
    relay(4)
    near(2)
    full(1)
    relay(5)
    near(3)
    near(4)
    relay(6)
    near(5)
    relay(7)
    near(6)
    near(7)
    projected(y_up)
    projected(y_down)
    opposite(2)
    opposite(3)
    backward(y_up)
    finish(2)
    finish(3)
    opposite(4)
    opposite(5)
    backward(y_down)
    opposite(6)
    opposite(7)
    for j in range(4, NC):
        finish(j)
    projected(y_opp)
    def send_kv(kb):
        rows = pl.ds(kb * B, B)
        dkb[rows] = (dKa[rows] * SCALE).astype(BF16)
        dvb[rows] = dVa[rows].astype(BF16)
        for c in range(2):
            g = kb * 2 + c

            @pl.when(me != g)
            def _():
                remote(dkb.at[rows_of(g)], dk_o.at[:, my_d], s_dk, r_dk, seq_dev(g)).start()
                remote(dvb.at[rows_of(g)], dv_o.at[:, my_d], s_dv, r_dv, seq_dev(g)).start()

    for kb in range(1, NB):

        @pl.when((kb > y_opp) & (kb != Y))
        def _():
            send_kv(kb)

    backward(y_opp)
    for kb in range(NB):

        @pl.when((kb <= y_opp) | (kb == Y))
        def _():
            send_kv(kb)

    own_dk = pltpu.make_async_copy(dkb.at[my_rows], dk_o.at[:, my_d], l_dk)
    own_dv = pltpu.make_async_copy(dvb.at[my_rows], dv_o.at[:, my_d], l_dv)
    own_dk.start()
    own_dv.start()

    chunk_at = {(CHUNK_X[j], CHUNK_OWN[j]): j for j in range(NC)}
    own_cols = pl.ds(mult(par * 256, 256), 256)

    def z_sum(dx):
        pltpu.make_async_copy(rz.at[dx], rz.at[dx], r_z.at[dx]).wait()
        s = Wb[chunk_at[dx, 1], XR:, own_cols].astype(F32)
        for i in range(3):
            s += rz[dx, i].astype(F32)
        if dx:
            s2b[dx - 1] = s.astype(BF16)
            remote(
                s2b.at[dx - 1], rz2.at[dx - 1], s_z2, r_z2, grid_dev(lax.rem(X + dx, 4), Z)
            ).start()
        else:
            fin[...] = s

    def x_sum(e):
        pltpu.make_async_copy(rx.at[e], rx.at[e], r_x.at[e]).wait()
        s = Wb[chunk_at[0, e], :XR].astype(F32)
        for i in range(3):
            s += rx[e, i].astype(F32)
        s1b[e] = s.astype(BF16)
        if e:
            sends = [(mult((1 - par) * 256, 256), Z + 1 - 2 * par)]
        else:
            sends = [(c * 256, 2 * other + c) for c in range(2)]
        for col, zz in sends:
            remote(
                s1b.at[e, :, pl.ds(col, 256)], rx2.at[z_slot(zz)], s_x2, r_x2, grid_dev(X, zz)
            ).start()

    z_sum(2)
    x_sum(0)
    z_sum(1)
    z_sum(3)
    x_sum(1)
    z_sum(0)
    pltpu.make_async_copy(rx2, rx2, r_x2).wait()
    norm = 1.0 / math.sqrt(T * 16)
    s = s1b[1, :, own_cols].astype(F32)
    for i in range(3):
        s += rx2[i].astype(F32)
    wg_o[:XR] = s * norm
    pltpu.make_async_copy(rz2, rz2, r_z2).wait()
    s = fin[...]
    for i in range(3):
        s += rz2[i].astype(F32)
    wg_o[XR:] = s * norm

    def drain(ref, *sems):
        for sem in sems:
            pltpu.make_async_copy(ref, ref, sem).wait()

    own_dq.wait()
    own_dk.wait()
    own_dv.wait()
    drain(qs.at[pl.ds(0, 7 * R)], s_q, s_dq, r_dq)
    drain(ks.at[pl.ds(0, 7 * R)], s_k, s_v, s_dk, s_dv, r_dk, r_dv)
    drain(G.at[pl.ds(0, 7)], s_ag)
    drain(rx, s_x)
    drain(rz, s_z)
    drain(rx2, s_x2)
    drain(rz2, s_z2)


def write_out(a, b, c, d, ao, bo, co, do, sem):
    copies = [
        pltpu.make_async_copy(src, dst, sem.at[i])
        for i, (src, dst) in enumerate(((a, ao), (b, bo), (c, co), (d, do)))
    ]
    for copy in copies:
        copy.start()
    for copy in copies:
        copy.wait()


def body(grad_out, queries, keys, values, out_weight, doc_starts):
    vm = pltpu.VMEM
    dma = pltpu.SemaphoreType.DMA
    hbm = pl.BlockSpec(memory_space=pl.ANY)
    scratch = [
        vm((T, F), BF16),
        vm((T, DH), BF16),
        vm((T, DH), BF16),
        vm((DH, T), BF16),
        vm((DH, T), BF16),
        vm((NC, T, CW), BF16),
        vm((NC, F, CW), BF16),
        vm((H, NB, T, B), BF16),
        vm((F, T), BF16),
        vm((NB, T, B), F32),
        vm((T, F), F32),
        vm((T, F), BF16),
        vm((NC - EARLY, F, CW), F32),
        vm((NC, F, CW), BF16),
        vm((2, 3, XR, 512), BF16),
        vm((4, 3, ZR, 256), BF16),
        vm((2, XR, 512), BF16),
        vm((3, ZR, 256), BF16),
        vm((3, XR, 256), BF16),
        vm((3, ZR, 256), BF16),
        vm((ZR, 256), F32),
        vm((NB, B, F), BF16),
        vm((T, DH), F32),
        vm((T, DH), F32),
        vm((T, DH), BF16),
        vm((T, DH), BF16),
    ]
    scratch += [dma] * 9
    scratch += [dma] + [dma((NC,))] * 6 + [dma] * 2
    scratch += [dma] * 6 + [dma((2,)), dma((4,))]
    scratch += [dma] * 9
    shapes = (((R, D), BF16), ((R, 1024), BF16), ((R, 1024), BF16), ((F, 256), F32))
    local = pl.BlockSpec(memory_space=pltpu.VMEM)
    held = pl.pallas_call(
        kernel,
        name="attention_back",
        out_shape=tuple(vm(shape, dtype) for shape, dtype in shapes),
        in_specs=[hbm] * 5 + [pl.BlockSpec(memory_space=pltpu.SMEM)],
        out_specs=(local,) * 4,
        scratch_shapes=scratch,
        compiler_params=pltpu.CompilerParams(
            collective_id=0, has_side_effects=True, vmem_limit_bytes=60 * 1024 * 1024
        ),
    )(grad_out[0], queries[0], keys[0], values[0], out_weight, doc_starts)
    out = pl.pallas_call(
        write_out,
        name="write_out",
        out_shape=tuple(jax.ShapeDtypeStruct(shape, dtype) for shape, dtype in shapes),
        in_specs=[local] * 4,
        out_specs=(hbm,) * 4,
        scratch_shapes=[dma((4,))],
    )(*[pltpu.with_memory_space_constraint(x, pltpu.VMEM) for x in held])
    return (out[0][None], out[1][None], out[2][None], out[3])


def solution(mesh):
    return jax.shard_map(
        body,
        mesh=mesh,
        in_specs=(
            P("dp", "seq", None),
            P("dp", "seq", None),
            P("dp", "seq", None),
            P("dp", "seq", None),
            P("seq", None),
            P("dp", None),
        ),
        out_specs=(
            P("dp", "seq", None),
            P("dp", "seq", None),
            P("dp", "seq", None),
            P("seq", "dp"),
        ),
        check_vma=False,
    )
```
